32 devices in a mesh: seq: 8 (over z, y), tensor: 4 (over x, core).
Axes of the slice: x: 2, y: 2, z: 4, core: 2. Of those that a mesh axis runs over, the one named last changes fastest.
Arguments:
- inputs: bfloat16 [2, 2048, 1536], P(None, 'seq'), may hold values from -6 to 6
- text_states: bfloat16 [2, 1536, 1536], P(None, 'seq'), may hold values from -6 to 6
- timestep_emb: float32 [2, 3, 6, 1536], replicated, may hold values from -3 to 3
- modulation: float32 [6, 1536], replicated, may hold values from -3 to 3
- attn_in: bfloat16 [3, 1536, 1536], P(None, 'seq', 'tensor'), may hold values from -0.15625 to 0.15625
- in_bias: bfloat16 [2, 3, 1536], P(None, None, 'tensor'), may hold values from -2 to 2
- norm_gains: bfloat16 [4, 1536], P(None, 'tensor'), may hold values from 0.5 to 1.5
- attn_out: bfloat16 [1536, 1536], P('tensor', 'seq'), may hold values from -0.625 to 0.625
- cross_in: bfloat16 [3, 1536, 1536], P(None, 'seq', 'tensor'), may hold values from -0.15625 to 0.15625
- cross_out: bfloat16 [1536, 1536], P('tensor', 'seq'), may hold values from -0.625 to 0.625
- cross_norm_gain: bfloat16 [1536], replicated, may hold values from 0.5 to 1.5
- cross_norm_bias: bfloat16 [1536], replicated, may hold values from -2 to 2
- ffn_in: bfloat16 [1536, 8960], P('seq', 'tensor'), may hold values from -0.15625 to 0.15625
- ffn_bias: bfloat16 [8960], P('tensor'), may hold values from -2 to 2
- ffn_out: bfloat16 [8960, 1536], P('tensor', 'seq'), may hold values from -0.0625 to 0.0625
- out_bias: bfloat16 [3, 1536], replicated, may hold values from -2 to 2
- latent_ids: int32 [2, 2048], P(None, 'seq'), may hold values from 0 to 2, never falling along the last dimension, each value on 1 to 1536 neighbouring positions
- pad_mask: int32 [2, 2048], P(None, 'seq'), may hold values 0 or 1
- frame_pos: int32 [2, 2048], P(None, 'seq'), may hold values from 0 to 7
- row_pos: int32 [2, 2048], P(None, 'seq'), may hold values from 0 to 14
- col_pos: int32 [2, 2048], P(None, 'seq'), may hold values from 0 to 25
- cotangent: bfloat16 [2, 2048, 1536], P(None, 'seq'), may hold values from -6 to 6
Outputs:
- block_out: bfloat16 [2, 2048, 1536], P(None, 'seq')
- grad_inputs: float32 [2, 2048, 1536], P(None, 'seq')
- grad_text: float32 [2, 1536, 1536], P(None, 'seq')
- grad_timestep: float32 [2, 3, 6, 1536], replicated
- grad_modulation: float32 [6, 1536], replicated
- grad_attn_in: float32 [3, 1536, 1536], P(None, 'seq', 'tensor')
- grad_in_bias: float32 [2, 3, 1536], P(None, None, 'tensor')
- grad_norm_gains: float32 [4, 1536], P(None, 'tensor')
- grad_attn_out: float32 [1536, 1536], P('tensor', 'seq')
- grad_cross_in: float32 [3, 1536, 1536], P(None, 'seq', 'tensor')
- grad_cross_out: float32 [1536, 1536], P('tensor', 'seq')
- grad_cross_gain: float32 [1536], replicated
- grad_cross_bias: float32 [1536], replicated
- grad_ffn_in: float32 [1536, 8960], P('seq', 'tensor')
- grad_ffn_bias: float32 [8960], P('tensor')
- grad_ffn_out: float32 [8960, 1536], P('tensor', 'seq')
- grad_out_bias: float32 [3, 1536], replicated
The draws below stay inside these ranges and needn't reach their ends.
Inputs may be any that keep to these rules, and one draw needn't show every extreme that they name: `latent_ids`: within each micro-batch the latent numbers never fall along the tokens; every latent has 1 to 1536 tokens and one has exactly 1536.
All inputs are finite; a program needn't handle non-finite values. No bound on the sum of `pad_mask` on one device may be relied on, other than what follows from the above.
Results may differ from the reference program's by a relative error of at most 0.025.
Values may be sent and summed in bfloat16 or wider, within the bound.
No kernel may reach another device: no remote copies, remote signals or barrier semaphores. Data moves between devices by JAX's collectives and lax.ppermute only.
A program may use at most 256 MiB of HBM per device.

```python
import math
import jax
import jax.numpy as jnp
import numpy as np
from jax import lax

D = 1536
HEADS = 12
FF = 8960
HD = 128
TXT = 512
MICRO = 2
LATENTS = 3
TOKENS = 2048
LAT_MOST = 1536
TEXTS = 1536
KEY_BLOCK = 512


def place_ends(values, rng, least, largest):
    index_at = [jax.random.randint(jax.random.fold_in(rng, axis), (), 0, length) for axis, length in enumerate(values.shape)]
    longest = values.shape.index(max(values.shape))
    beside = index_at[:longest] + [(index_at[longest] + 1) % values.shape[longest]] + index_at[longest + 1:]
    return values.at[tuple(index_at)].set(least).at[tuple(beside)].set(largest)


def block_levels(stream_key, dims, cuts, smallest, high):
    def one(axis_at, blocks):
        heights = jax.random.uniform(jax.random.fold_in(jax.random.fold_in(stream_key, 6), axis_at), (blocks,), jnp.float32, smallest / len(cuts), high / len(cuts))
        return jnp.repeat(jnp.exp(heights), dims[axis_at] // blocks).reshape((-1,) + (1,) * (len(dims) - axis_at - 1))

    level = one(*cuts[0])
    for cut in cuts[1:]:
        level = level * one(*cut)
    return level


def split_up(amount, total, bound, slope):
    portions = [(1 << 20) // math.isqrt(rank ** slope) + 1 for rank in range(2, amount + 1)]
    surplus, counts = total - bound - (amount - 1), [1] * (amount - 1)
    while surplus > 0:
        candidates = [i for i in range(amount - 1) if counts[i] < bound]
        whole, remaining = sum([portions[i] for i in candidates]), surplus
        for i in candidates:
            addition = min(bound - counts[i], max(1, remaining * portions[i] // whole), surplus)
            counts[i] = counts[i] + addition
            surplus = surplus - addition
    return np.array([bound] + counts)


def ragged(own_key, amount, total, limit, skew):
    if amount == 2:
        one = jax.random.randint(own_key, (), max(1, total - limit), min(limit, total - 1) + 1)
        return jnp.stack([one, total - one])
    tallies = jnp.asarray(split_up(amount, total, limit, skew), jnp.int32)
    pairs = (amount - 1) // 2
    donor, receiver = tallies[1:1 + 2 * pairs:2], tallies[2:2 + 2 * pairs:2]
    room = jnp.minimum(donor - 1, limit - receiver)
    passed = jax.random.randint(jax.random.fold_in(own_key, 1), (pairs,), 0, 1 << 20) % (room + 1)
    tallies = tallies.at[1:1 + 2 * pairs:2].set(donor - passed).at[2:2 + 2 * pairs:2].set(receiver + passed)
    return tallies[jax.random.permutation(jax.random.fold_in(own_key, 2), amount)]


def centred(stream_key, shape, spread, limit, split=(), kind=jnp.bfloat16):
    level = block_levels(stream_key, shape, split, -0.22, 0.18) if split else 1.0
    values = jax.random.normal(stream_key, shape, jnp.float32) * spread * level
    return jnp.minimum(jnp.maximum(values, -limit), limit).astype(kind)


def setup_inputs(seed: int = 0) -> dict:
    key_list = jax.random.split(jax.random.key(seed), 23)
    return {
        "inputs": centred(key_list[0], (MICRO, TOKENS, D), 1.0, 6.0, ((1, 8),)),
        "text_states": centred(key_list[1], (MICRO, TEXTS, D), 1.0, 6.0, ((1, 8),)),
        "timestep_emb": centred(key_list[2], (MICRO, LATENTS, 6, D), 0.5, 3.0, (), jnp.float32),
        "modulation": centred(key_list[3], (6, D), 0.5, 3.0, (), jnp.float32),
        "attn_in": centred(key_list[4], (3, D, D), D ** -0.5, 0.15625, ((1, 8), (2, 4))),
        "in_bias": centred(key_list[5], (2, 3, D), 0.3, 2.0, ((2, 4),)),
        "norm_gains": jnp.clip(1.0 + 0.1 * jax.random.normal(key_list[6], (4, D), jnp.float32), 0.5, 1.5).astype(jnp.bfloat16),
        "attn_out": centred(key_list[7], (D, D), (D // 16) ** -0.5, 0.625, ((0, 4), (1, 8))),
        "cross_in": centred(key_list[8], (3, D, D), D ** -0.5, 0.15625, ((1, 8), (2, 4))),
        "cross_out": centred(key_list[9], (D, D), (D // 16) ** -0.5, 0.625, ((0, 4), (1, 8))),
        "cross_norm_gain": jnp.clip(1.0 + 0.1 * jax.random.normal(key_list[10], (D,), jnp.float32), 0.5, 1.5).astype(jnp.bfloat16),
        "cross_norm_bias": centred(key_list[11], (D,), 0.3, 2.0),
        "ffn_in": centred(key_list[12], (D, FF), D ** -0.5, 0.15625, ((0, 8), (1, 4))),
        "ffn_bias": centred(key_list[13], (FF,), 0.3, 2.0, ((0, 4),)),
        "ffn_out": centred(key_list[14], (FF, D), FF ** -0.5, 0.0625, ((0, 4), (1, 8))),
        "out_bias": centred(key_list[15], (3, D), 0.3, 2.0),
        "latent_ids": jax.vmap(lambda own: jnp.searchsorted(jnp.cumsum(ragged(own, LATENTS, TOKENS, LAT_MOST, 1)), jnp.arange(TOKENS), side="right"))(jax.random.split(key_list[16], MICRO)).reshape((MICRO, TOKENS)).astype(jnp.int32),
        "pad_mask": place_ends((jax.random.randint(key_list[17], (MICRO, TOKENS), 0, 8) < 7).astype(jnp.int32), jax.random.fold_in(key_list[17], 1), 0, 1),
        "frame_pos": place_ends(jax.random.randint(key_list[18], (MICRO, TOKENS), 0, 8), jax.random.fold_in(key_list[18], 1), 0, 7).astype(jnp.int32),
        "row_pos": place_ends(jax.random.randint(key_list[19], (MICRO, TOKENS), 0, 15), jax.random.fold_in(key_list[19], 1), 0, 14).astype(jnp.int32),
        "col_pos": place_ends(jax.random.randint(key_list[20], (MICRO, TOKENS), 0, 26), jax.random.fold_in(key_list[20], 1), 0, 25).astype(jnp.int32),
        "cotangent": centred(key_list[21], (MICRO, TOKENS, D), 1.0, 6.0, ((1, 8),)),
    }


@jax.custom_vjp
def low(v):
    return lax.optimization_barrier(v.astype(jnp.bfloat16)).astype(jnp.float32)

@jax.custom_vjp
def low_back(v):
    return v

def low_keep(v):
    return (low(v), None)

def low_pass(kept, grad):
    return (grad,)

def back_keep(v):
    return (v, None)

def back_low(kept, grad):
    return (low(grad),)
low.defvjp(low_keep, low_pass)
low_back.defvjp(back_keep, back_low)
EPS = 1e-06
HIGH = lax.Precision.HIGHEST

def norm_plain(values):
    center = values - lax.optimization_barrier(jnp.mean(values, -1, keepdims=True))
    return center * lax.rsqrt(lax.optimization_barrier(jnp.mean(center * center, -1, keepdims=True)) + EPS)

def rms_scale(values, gain):
    return values * lax.rsqrt(lax.optimization_barrier(jnp.mean(values * values, -1, keepdims=True)) + EPS) * gain

def rope_tables(frames, rows_pos, cols_pos, head_width):
    part_size = head_width // 6
    widths = (head_width - 4 * part_size, 2 * part_size, 2 * part_size)
    angles = []
    for position, group_width in zip((frames, rows_pos, cols_pos), widths):
        exponent = jnp.arange(0, group_width, 2).astype(jnp.float32) / group_width
        angles.append(position.astype(jnp.float32)[:, None] * jnp.power(10000.0, -exponent)[None, :])
    joined = jnp.concatenate(angles, -1)
    return (jnp.cos(joined), jnp.sin(joined))

def rotate(values, cosine, sine):
    shape = values.shape
    pairs = values.reshape(shape[:-1] + (shape[-1] // 2, 2))
    first = pairs[..., 0]
    second = pairs[..., 1]
    cosine = cosine[:, None, :]
    sine = sine[:, None, :]
    return jnp.stack((first * cosine - second * sine, first * sine + second * cosine), -1).reshape(shape)

def attention(queries, key_rows, value_rows, query_group, key_group, key_keep):
    rows_all = queries.shape[0]
    factor = 1.0 / math.sqrt(HD)
    key_index = jnp.arange(key_rows.shape[0], dtype=jnp.int32)

    def block_fn(packed):
        query_block, group_block, index_block = packed
        scores = low_back(jnp.einsum('qhd,khd->hqk', query_block, key_rows, precision=HIGH) * factor)
        allowed = (group_block[:, None] == key_group[None, :]) & ((key_keep[None, :] == 1) | (index_block[:, None] == key_index[None, :]))
        probs = jax.nn.softmax(jnp.where(allowed[None], scores, -1e+30), axis=-1)
        return jnp.einsum('hqk,khd->qhd', low(probs), value_rows, precision=HIGH)
    blocks = rows_all // KEY_BLOCK
    packed = (queries.reshape((blocks, KEY_BLOCK) + queries.shape[1:]), query_group.reshape(blocks, KEY_BLOCK), jnp.arange(rows_all, dtype=jnp.int32).reshape(blocks, KEY_BLOCK))
    return lax.map(jax.checkpoint(block_fn), packed).reshape(queries.shape)

def reference(inputs, text_states, timestep_emb, modulation, attn_in, in_bias, norm_gains, attn_out, cross_in, cross_out, cross_norm_gain, cross_norm_bias, ffn_in, ffn_bias, ffn_out, out_bias, latent_ids, pad_mask, frame_pos, row_pos, col_pos, cotangent):
    floats = tuple((array.astype(jnp.float32) for array in (inputs, text_states, timestep_emb, modulation, attn_in, in_bias, norm_gains, attn_out, cross_in, cross_out, cross_norm_gain, cross_norm_bias, ffn_in, ffn_bias, ffn_out, out_bias)))
    tables = [rope_tables(frame_pos[index_mb], row_pos[index_mb], col_pos[index_mb], HD) for index_mb in range(MICRO)]
    group_text = jnp.arange(TEXTS, dtype=jnp.int32) // TXT
    keep_text = jnp.ones((TEXTS,), jnp.int32)

    def forward(state_all, text_all, temb_all, mod_table, proj_in, bias_in, gains, proj_out, cproj_in, cproj_out, cgain, cbias, up_weight, up_bias, down_weight, bias_out):
        results = []
        for index_mb in range(MICRO):
            ids_here = latent_ids[index_mb]
            shifts = (mod_table[None] + temb_all[index_mb])[ids_here]
            state_in = state_all[index_mb]
            act = low(norm_plain(state_in) * (1.0 + shifts[:, 1]) + shifts[:, 0])
            projected = jnp.einsum('td,sdc->stc', act, proj_in, precision=HIGH) + bias_in[0][:, None, :]
            query_norm = rms_scale(low_back(projected[0]), gains[0])
            key_norm = rms_scale(low_back(projected[1]), gains[1])
            value_rows = low(low_back(projected[2])).reshape(TOKENS, HEADS, HD)
            cosine, sine = tables[index_mb]
            query_rows = low(rotate(query_norm.reshape(TOKENS, HEADS, HD), cosine, sine))
            key_rows = low(rotate(key_norm.reshape(TOKENS, HEADS, HD), cosine, sine))
            attended = low(low_back(attention(query_rows, key_rows, value_rows, ids_here, ids_here, pad_mask[index_mb]))).reshape(TOKENS, D)
            branch_one = low_back(jnp.dot(attended, proj_out, precision=HIGH, preferred_element_type=jnp.float32) + bias_out[0])
            state_one = state_in + branch_one * shifts[:, 2]
            cross_act = low(norm_plain(state_one) * cgain + cbias)
            cquery = low(rms_scale(low_back(jnp.dot(cross_act, cproj_in[0], precision=HIGH, preferred_element_type=jnp.float32) + bias_in[1, 0]), gains[2])).reshape(TOKENS, HEADS, HD)
            text_here = text_all[index_mb]
            ckey = low(rms_scale(low_back(jnp.dot(text_here, cproj_in[1], precision=HIGH, preferred_element_type=jnp.float32) + bias_in[1, 1]), gains[3])).reshape(TEXTS, HEADS, HD)
            cvalue = low(low_back(jnp.dot(text_here, cproj_in[2], precision=HIGH, preferred_element_type=jnp.float32) + bias_in[1, 2])).reshape(TEXTS, HEADS, HD)
            crossed = low(low_back(attention(cquery, ckey, cvalue, ids_here, group_text, keep_text))).reshape(TOKENS, D)
            branch_two = low_back(jnp.dot(crossed, cproj_out, precision=HIGH, preferred_element_type=jnp.float32) + bias_out[1])
            state_two = state_one + branch_two
            ffn_act = low(norm_plain(state_two) * (1.0 + shifts[:, 4]) + shifts[:, 3])
            hidden = low(jax.nn.gelu(low_back(jnp.dot(ffn_act, up_weight, precision=HIGH, preferred_element_type=jnp.float32) + up_bias), approximate=True))
            branch_three = low_back(jnp.dot(hidden, down_weight, precision=HIGH, preferred_element_type=jnp.float32) + bias_out[2])
            results.append(state_two + branch_three * shifts[:, 5])
        return jnp.stack(results)
    result, pull = jax.vjp(forward, *floats)
    grads = pull(cotangent.astype(jnp.float32))
    return (result.astype(jnp.bfloat16), grads[0], grads[1], grads[2], grads[3], grads[4], grads[5], grads[6], grads[7], grads[8], grads[9], grads[10], grads[11], grads[12], grads[13], grads[14], grads[15])
```

```python
from functools import partial
import math

import jax
import jax.numpy as jnp
from jax import lax
from jax.experimental import pallas as pl
from jax.experimental.pallas import tpu as pltpu
from jax.sharding import PartitionSpec as P

HD = 128
TXT = 512
EPS = 1e-06
HIGH = lax.Precision.HIGHEST
NEG = -1e30
F32 = jnp.float32
BF16 = jnp.bfloat16
AXES = ("seq", "tensor")


def norm_stats(values):
    center = values - jnp.mean(values, -1, keepdims=True)
    return center, lax.rsqrt(jnp.mean(center * center, -1, keepdims=True) + EPS)


def norm_plain(values):
    center, inverse = norm_stats(values)
    return center * inverse


def norm_back(values, cotangent):
    center, inverse = norm_stats(values)
    normed = center * inverse
    return inverse * (
        cotangent
        - jnp.mean(cotangent, -1, keepdims=True)
        - normed * jnp.mean(cotangent * normed, -1, keepdims=True)
    )


def nn(a, b):
    return lax.dot_general(a, b, (((1,), (0,)), ((), ())), preferred_element_type=F32)


def nt(a, b):
    return lax.dot_general(a, b, (((1,), (1,)), ((), ())), preferred_element_type=F32)


def tn(a, b):
    return lax.dot_general(a, b, (((0,), (0,)), ((), ())), preferred_element_type=F32)


def allowed_pairs(query_code, key_code, row_base, shape, transposed, diagonal):
    same = query_code == key_code
    if not diagonal:
        return same
    rows = lax.broadcasted_iota(jnp.int32, shape, 1 if transposed else 0) + row_base
    cols = lax.broadcasted_iota(jnp.int32, shape, 0 if transposed else 1)
    return same | (rows == cols)


def forward_kernel(
    query_ref, key_ref, value_ref, qcode_ref, kcode_ref, out_ref, total_ref, *, diagonal
):
    rows = query_ref.shape[0]
    count = key_ref.shape[0]
    mask = allowed_pairs(
        qcode_ref[...],
        kcode_ref[...],
        pl.program_id(0) * rows,
        (rows, count),
        False,
        diagonal,
    )
    factor = 1.0 / math.sqrt(HD)
    for head in range(query_ref.shape[1] // HD):
        cols = slice(head * HD, (head + 1) * HD)
        scores = jnp.where(mask, nt(query_ref[:, cols], key_ref[:, cols]) * factor, NEG)
        top = jnp.max(scores, -1, keepdims=True)
        weights = jnp.exp(scores - top)
        total = jnp.sum(weights, -1, keepdims=True)
        probs = (weights * (1.0 / total)).astype(BF16)
        out_ref[:, cols] = nn(probs, value_ref[:, cols]).astype(out_ref.dtype)
        total_ref[:, head : head + 1] = top + jnp.log(total)


def backward_kernel(
    query_ref,
    grad_ref,
    key_ref,
    value_ref,
    qcode_ref,
    kcode_ref,
    total_ref,
    dquery_ref,
    dkey_ref,
    dvalue_ref,
    key_sum,
    value_sum,
    *,
    diagonal,
):
    rows = query_ref.shape[0]
    count = key_ref.shape[0]
    step = pl.program_id(1)
    mask = allowed_pairs(
        qcode_ref[...],
        kcode_ref[...],
        step * rows,
        (count, rows),
        True,
        diagonal,
    )
    factor = 1.0 / math.sqrt(HD)

    @pl.when(step == 0)
    def _():
        key_sum[...] = jnp.zeros_like(key_sum)
        value_sum[...] = jnp.zeros_like(value_sum)

    for head in range(query_ref.shape[1] // HD):
        cols = slice(head * HD, (head + 1) * HD)
        query, grad = query_ref[:, cols], grad_ref[:, cols]
        key, value = key_ref[:, cols], value_ref[:, cols]
        scores = nt(key, query) * factor
        probs = jnp.where(mask, jnp.exp(scores - total_ref[head]), 0.0)
        dprobs = nt(value, grad)
        delta = jnp.sum(probs * dprobs, 0, keepdims=True)
        dscores = (probs * (dprobs - delta)).astype(BF16)
        value_sum[:, cols] += nn(probs.astype(BF16), grad)
        key_sum[:, cols] += nn(dscores, query)
        dquery_ref[:, cols] = tn(dscores, key) * factor

    @pl.when(step == pl.num_programs(1) - 1)
    def _():
        dkey_ref[...] = (key_sum[...] * factor).astype(BF16)
        dvalue_ref[...] = value_sum[...].astype(BF16)


def tile_rows(rows, count):
    tile = rows
    while tile > 128 and (tile * count > 256 * 2048) and tile % 2 == 0:
        tile //= 2
    return tile


def attend(queries, keys, values, query_code, key_code, diagonal):
    rows, width = queries.shape
    count = keys.shape[0]
    tile = tile_rows(rows, count)
    whole = lambda i: (0, 0)
    part = lambda i: (i, 0)
    return pl.pallas_call(
        partial(forward_kernel, diagonal=diagonal),
        grid=(rows // tile,),
        in_specs=[
            pl.BlockSpec((tile, width), part),
            pl.BlockSpec((count, width), whole),
            pl.BlockSpec((count, width), whole),
            pl.BlockSpec((tile, 1), part),
            pl.BlockSpec((1, count), whole),
        ],
        out_specs=[pl.BlockSpec((tile, width), part), pl.BlockSpec((tile, HD), part)],
        out_shape=[
            jax.ShapeDtypeStruct((rows, width), BF16),
            jax.ShapeDtypeStruct((rows, HD), F32),
        ],
        cost_estimate=pl.CostEstimate(
            flops=4 * rows * count * width,
            bytes_accessed=4 * (rows + count) * width,
            transcendentals=rows * count * (width // HD),
        ),
        compiler_params=pltpu.CompilerParams(vmem_limit_bytes=60 * 2**20),
        name="attend" if diagonal else "attend_text",
    )(queries, keys, values, query_code[:, None], key_code[None, :])


def attend_back(queries, grads, keys, values, query_code, key_code, totals, diagonal):
    rows, width = queries.shape
    count = keys.shape[0]
    tile = tile_rows(rows, count)
    heads = width // HD
    part_heads = heads if count * width <= 4096 * 3 * HD else 1
    cols = part_heads * HD
    whole = lambda h, i: (0, h)
    part = lambda h, i: (i, h)
    lines = totals[:, :heads].T[:, None, :]
    return pl.pallas_call(
        partial(backward_kernel, diagonal=diagonal),
        grid=(heads // part_heads, rows // tile),
        in_specs=[
            pl.BlockSpec((tile, cols), part),
            pl.BlockSpec((tile, cols), part),
            pl.BlockSpec((count, cols), whole),
            pl.BlockSpec((count, cols), whole),
            pl.BlockSpec((1, tile), lambda h, i: (0, i)),
            pl.BlockSpec((count, 1), lambda h, i: (0, 0)),
            pl.BlockSpec((part_heads, 1, tile), lambda h, i: (h, 0, i)),
        ],
        out_specs=[
            pl.BlockSpec((tile, cols), part),
            pl.BlockSpec((count, cols), whole),
            pl.BlockSpec((count, cols), whole),
        ],
        out_shape=[
            jax.ShapeDtypeStruct((rows, width), F32),
            jax.ShapeDtypeStruct((count, width), BF16),
            jax.ShapeDtypeStruct((count, width), BF16),
        ],
        scratch_shapes=[pltpu.VMEM((count, cols), F32), pltpu.VMEM((count, cols), F32)],
        cost_estimate=pl.CostEstimate(
            flops=10 * rows * count * width,
            bytes_accessed=8 * (rows + count) * width,
            transcendentals=rows * count * heads,
        ),
        compiler_params=pltpu.CompilerParams(vmem_limit_bytes=60 * 2**20),
        name="attend_back" if diagonal else "attend_text_back",
    )(queries, grads, keys, values, query_code[None, :], key_code[:, None], lines)


def rope_tables(frames, rows_pos, cols_pos):
    part_size = HD // 6
    widths = (HD - 4 * part_size, 2 * part_size, 2 * part_size)
    angles = []
    for position, group_width in zip((frames, rows_pos, cols_pos), widths):
        exponent = jnp.arange(0, group_width, 2).astype(F32) / group_width
        exponent = jnp.repeat(exponent, 2)
        angles.append(
            position.astype(F32)[:, None] * jnp.power(10000.0, -exponent)[None, :]
        )
    joined = jnp.concatenate(angles, -1)
    return jnp.cos(joined), jnp.sin(joined)


def rotate(values, cosine, sine):
    rows, width = values.shape
    low = lax.broadcasted_iota(jnp.int32, (width, width), 0)
    high = lax.broadcasted_iota(jnp.int32, (width, width), 1)
    turn = jnp.where(
        low == (high ^ 1), jnp.where(high % 2 == 0, -1.0, 1.0), 0.0
    ).astype(F32)
    heads = width // HD
    turned = jnp.dot(values, turn, precision=HIGH, preferred_element_type=F32)
    return values * jnp.tile(cosine, (1, heads)) + turned * jnp.tile(sine, (1, heads))


def shards(
    inputs,
    text_states,
    timestep_emb,
    modulation,
    attn_in,
    in_bias,
    norm_gains,
    attn_out,
    cross_in,
    cross_out,
    cross_norm_gain,
    cross_norm_bias,
    ffn_in,
    ffn_bias,
    ffn_out,
    out_bias,
    latent_ids,
    pad_mask,
    frame_pos,
    row_pos,
    col_pos,
    cotangent,
):
    micros, tok_rows, width = inputs.shape
    text_rows = text_states.shape[1]
    latents = timestep_emb.shape[1]
    columns = attn_in.shape[2]
    hidden = ffn_in.shape[1]
    slice_rows = attn_in.shape[1]
    seq_size, tensor_size = lax.axis_size("seq"), lax.axis_size("tensor")
    places = seq_size * tensor_size
    bits = seq_size.bit_length() - 1
    s, t = lax.axis_index("seq"), lax.axis_index("tensor")
    top = bits - 1
    rest = [b for b in range(bits) if b not in (1, top)]

    def seq_bit(b):
        return (s >> b) & 1

    k, w, x, c = seq_bit(top), seq_bit(1), t >> 1, t & 1
    own_slice = (s & ~2) | (c << 1)
    hop_c, hop_x, hop_w, hop_k = 1, 2, tensor_size << 1, tensor_size << top
    hop_rest = [tensor_size << b for b in rest]
    hop_group = [0, hop_x, hop_w, hop_x | hop_w]

    def hop(value, mask):
        return lax.ppermute(value, AXES, [(d, d ^ mask) for d in range(places)])

    def swap(value):
        def other(d):
            low, high = d & 1, (d // hop_w) & 1
            return d if low == high else d ^ 1 ^ hop_w

        return lax.ppermute(value, AXES, [(d, other(d)) for d in range(places)])

    def gather_weight(block):
        held = [(0, swap(block))]
        for mask, offset in (
            [(hop_k, 1 << top)]
            + [(m, 1 << b) for m, b in zip(hop_rest, rest)]
            + [(hop_c, 2)]
        ):
            held = held + [(o | offset, hop(v, mask)) for o, v in held]
        out = jnp.zeros((seq_size,) + block.shape, block.dtype)
        for offset, value in held:
            out = lax.dynamic_update_index_in_dim(out, value, own_slice ^ offset, 0)
        return out.reshape(seq_size * block.shape[0], block.shape[1])

    def scatter_weight(grad):
        cols = grad.shape[1]
        current = grad.astype(BF16).reshape((2,) * bits + (slice_rows, cols))
        for mask, b, mine in (
            [(hop_c, 1, c)]
            + [(m, b, seq_bit(b)) for m, b in zip(hop_rest, rest)]
            + [(hop_k, top, k)]
        ):
            axis = bits - 1 - b
            given = lax.dynamic_index_in_dim(current, 1 - mine, axis, keepdims=True)
            kept = lax.dynamic_index_in_dim(current, mine, axis, keepdims=True)
            current = (kept.astype(F32) + hop(given, mask).astype(F32)).astype(BF16)
        return swap(current.reshape(slice_rows, cols))

    def gather_tokens(value):
        for mask in hop_rest + [hop_c]:
            value = jnp.concatenate((value, hop(value, mask)), 0)
        return value

    def scatter_tokens(value):
        for mask in [hop_c] + hop_rest[::-1]:
            half = value.shape[0] // 2
            value = (
                value[:half].astype(F32) + hop(value[half:], mask).astype(F32)
            ).astype(BF16)
        return value

    def spread(value):
        return jnp.concatenate([value] + [hop(value, m) for m in hop_group[1:]], 0)

    def collect(value):
        parts = value.astype(BF16).reshape(4, value.shape[0] // 4, value.shape[1])
        total = parts[0].astype(F32)
        for j in (1, 2, 3):
            total = total + hop(parts[j], hop_group[j]).astype(F32)
        return total

    def group_sum(value, flips):
        rows = value.shape[-1]
        total = value
        for j in (1, 2, 3):
            other = hop(value, hop_group[j])
            shift = flips(j)
            if shift:
                count = 4 if flips(1) else 2
                size = rows // count
                order = [i ^ shift for i in range(count)]
                other = jnp.concatenate(
                    [other[..., i * size : (i + 1) * size] for i in order], -1
                )
            total = total + other
        return total

    def token_sum(value):
        return group_sum(value, lambda j: j)

    def text_sum(value):
        return group_sum(value, lambda j: j >> 1)

    def all_sum(value, masks):
        for mask in masks:
            value = value.astype(BF16)
            value = value.astype(F32) + hop(value, mask).astype(F32)
        return value

    def by_home(own, other):
        return jnp.where(c == w, own, other)

    pack = lambda a: a.transpose(1, 0, 2).reshape(slice_rows, -1)
    w_attn = gather_weight(pack(attn_in))
    w_text = gather_weight(pack(cross_in[1:]))
    w_mid = gather_weight(jnp.concatenate((attn_out.T, cross_in[0], cross_out.T), 1))
    w_attn_out = w_mid[:, :columns]
    w_cross_q = w_mid[:, columns : 2 * columns]
    w_cross_out = w_mid[:, 2 * columns :]
    w_up = gather_weight(ffn_in)
    w_down = gather_weight(ffn_out.T)

    flat = jnp.concatenate((in_bias.reshape(-1), norm_gains.reshape(-1), ffn_bias))
    flat = by_home(flat, hop(flat, hop_c)).astype(F32)
    bias_in = flat[: 6 * columns].reshape(2, 3, columns)
    gains = flat[6 * columns : 10 * columns].reshape(4, columns)
    bias_ffn = flat[10 * columns :]
    bias_out = out_bias.astype(F32)
    cgain = cross_norm_gain.astype(F32)
    cbias = cross_norm_bias.astype(F32)

    meta = jnp.stack((latent_ids, pad_mask, frame_pos, row_pos, col_pos))[None]
    for mask in [hop_k, hop_w] + hop_rest:
        meta = jnp.concatenate((meta, hop(meta, mask)), 0)
    meta = lax.dynamic_index_in_dim(meta, k, 2, keepdims=False)
    piece = tok_rows // 4
    meta = meta.reshape((2,) * bits + (5, 2, 2, piece))
    meta = jnp.where(x == 1, jnp.flip(meta, bits + 1), meta)
    meta = jnp.where(c == 1, jnp.flip(meta, bits + 2), meta)
    others = list(range(bits - 2))
    meta = meta.transpose([bits, bits + 2] + others + [bits - 2, bits + 1, bits - 1, bits + 3])
    meta = meta.reshape(5, -1)
    group_rows = 8 * piece
    share_rows = 2 * piece
    ids_all = meta[0]
    key_code = jnp.where(meta[1] == 1, ids_all, -1)
    ids_here = ids_all[:group_rows]
    ids_share = ids_here[:share_rows, None]
    cosine, sine = rope_tables(*(meta[i, :group_rows] for i in (2, 3, 4)))

    def take_share(array):
        parts = array.reshape(micros, 4, piece, width)
        own = lax.dynamic_index_in_dim(
            lax.dynamic_index_in_dim(parts, k, 0, keepdims=False), t, 0, keepdims=False
        )
        given = lax.dynamic_index_in_dim(
            lax.dynamic_index_in_dim(parts, 1 - k, 0, keepdims=False), t, 0, keepdims=False
        )
        return jnp.concatenate((own, hop(given, hop_k)), 0).astype(F32)

    def give_back(share, rows_each, order):
        own, far = share[:rows_each], hop(share[rows_each:], hop_k)
        both = jnp.where(k == 0, jnp.stack((own, far)), jnp.stack((far, own)))
        across = hop(both, hop_x)
        pieces = ((0, both), (1, hop(both, hop_c)), (2, across), (3, hop(across, hop_c)))
        out = jnp.zeros((micros, 4, rows_each, width), both.dtype)
        for offset, value in pieces:
            out = lax.dynamic_update_index_in_dim(out, value, order(t ^ offset), 1)
        return out.reshape(micros, 4 * rows_each, width)

    state_in = take_share(inputs)
    grad_top = take_share(cotangent)
    table = modulation + lax.dynamic_index_in_dim(timestep_emb, k, 0, keepdims=False)

    def shift(number):
        out = table[0, number][None]
        for latent in range(1, latents):
            out = jnp.where(ids_share == latent, table[latent, number][None], out)
        return out

    half = text_rows // 2
    texts = text_states.reshape(micros, 2, half, width)

    def text_of(micro):
        return lax.dynamic_index_in_dim(
            lax.dynamic_index_in_dim(texts, micro, 0, keepdims=False), c, 0, keepdims=False
        )

    text_here = jnp.concatenate((text_of(k), hop(text_of(1 - k), hop_k)), 0)
    text_here = jnp.concatenate((text_here, hop(text_here, hop_w)), 0)
    number = jnp.arange(4 * half * seq_size // 2, dtype=jnp.int32)
    row, blocks = number % half, number // half
    row_k, row_w, row_rest = blocks & 1, (blocks >> 1) & 1, blocks >> 2
    place = ((row_k ^ k) << top) | ((row_w ^ w) << 1)
    for i, b in enumerate(rest):
        place = place | ((((row_rest >> i) & 1) ^ seq_bit(b)) << b)
    row_c = (row_rest >> len(rest)) ^ c
    text_code = (place * text_rows + row_c * half + row) // TXT

    normed_one = norm_plain(state_in)
    act_low = spread((normed_one * (1.0 + shift(1)) + shift(0)).astype(BF16))
    grad_branch_three_share = (grad_top * shift(5)).astype(BF16)
    grad_branch_three = spread(grad_branch_three_share)
    projected = nn(act_low, w_attn) + bias_in[0].reshape(1, -1)
    query_pre = projected[:, :columns]
    key_pre = projected[:, columns : 2 * columns]
    value_low = projected[:, 2 * columns :].astype(BF16)
    sums = token_sum(
        jnp.stack((jnp.sum(query_pre * query_pre, -1), jnp.sum(key_pre * key_pre, -1)))
    )
    inverse_q, inverse_k = lax.rsqrt(sums / width + EPS)[:, :, None]
    query_low = rotate(query_pre * inverse_q * gains[0], cosine, sine).astype(BF16)
    key_low = rotate(key_pre * inverse_k * gains[1], cosine, sine).astype(BF16)
    pair_all = gather_tokens(jnp.concatenate((key_low, value_low), 1))
    key_all, value_all = pair_all[:, :columns], pair_all[:, columns:]
    attn_low, total_self = attend(query_low, key_all, value_all, ids_here, key_code, True)
    branch_one = collect(nt(attn_low, w_attn_out)) + bias_out[0]
    state_one = state_in + branch_one * shift(2)

    text_pre = nn(text_here, w_text) + bias_in[1, 1:].reshape(1, -1)
    ckey_pre = text_pre[:, :columns]
    inverse_ck = lax.rsqrt(
        text_sum(jnp.sum(ckey_pre * ckey_pre, -1)[None])[0] / width + EPS
    )[:, None]
    ckey_low = (ckey_pre * inverse_ck * gains[3]).astype(BF16)
    cpair_all = gather_tokens(
        jnp.concatenate((ckey_low, text_pre[:, columns:].astype(BF16)), 1)
    )
    ckey_all, cvalue_all = cpair_all[:, :columns], cpair_all[:, columns:]

    normed_three = norm_plain(state_one)
    cross_act = spread((normed_three * cgain + cbias).astype(BF16))
    cquery_pre = nn(cross_act, w_cross_q) + bias_in[1, 0]
    inverse_cq = lax.rsqrt(
        token_sum(jnp.sum(cquery_pre * cquery_pre, -1)[None])[0] / width + EPS
    )[:, None]
    cquery_low = (cquery_pre * inverse_cq * gains[2]).astype(BF16)
    cross_low, total_cross = attend(
        cquery_low, ckey_all, cvalue_all, ids_here, text_code, False
    )
    branch_two = collect(nt(cross_low, w_cross_out)) + bias_out[1]
    state_two = state_one + branch_two

    normed_two = norm_plain(state_two)
    ffn_act = spread((normed_two * (1.0 + shift(4)) + shift(3)).astype(BF16))
    hidden_pre = nn(ffn_act, w_up) + bias_ffn
    hidden_low = jax.nn.gelu(hidden_pre, approximate=True).astype(BF16)
    branch_three = collect(nt(hidden_low, w_down)) + bias_out[2]
    out_share = (state_two + branch_three * shift(5)).astype(BF16)

    gelu_pull = jax.vjp(partial(jax.nn.gelu, approximate=True), hidden_pre)[1]
    grad_hidden = gelu_pull(nn(grad_branch_three, w_down))[0].astype(BF16)
    grad_ffn_act = collect(nt(grad_hidden, w_up))
    grad_up = scatter_weight(tn(ffn_act, grad_hidden))
    grad_down = scatter_weight(tn(grad_branch_three, hidden_low))
    grad_state_two = grad_top + norm_back(state_two, grad_ffn_act * (1.0 + shift(4)))

    grad_branch_two_share = grad_state_two.astype(BF16)
    grad_branch_two = spread(grad_branch_two_share)
    grad_cross = nn(grad_branch_two, w_cross_out).astype(BF16)
    grad_cquery, grad_ckey, grad_cvalue = attend_back(
        cquery_low,
        grad_cross,
        ckey_all,
        cvalue_all,
        ids_here,
        text_code,
        total_cross,
        False,
    )
    sums_cq = token_sum(jnp.sum(gains[2] * grad_cquery * cquery_pre, -1)[None])[0]

    def rms_back(pre, inverse, gain, cotangent_here, summed):
        scaled = inverse * inverse * inverse * summed[:, None] / width
        return (inverse * gain * cotangent_here - pre * scaled).astype(BF16)

    gcq_low = rms_back(cquery_pre, inverse_cq, gains[2], grad_cquery, sums_cq)
    grad_cross_act = collect(nt(gcq_low, w_cross_q))
    grad_state_one = grad_state_two + norm_back(state_one, grad_cross_act * cgain)

    gpair = scatter_tokens(jnp.concatenate((grad_ckey, grad_cvalue), 1))
    gckey = gpair[:, :columns].astype(F32)
    sums_ck = text_sum(jnp.sum(gains[3] * gckey * ckey_pre, -1)[None])[0]
    gck_low = rms_back(ckey_pre, inverse_ck, gains[3], gckey, sums_ck)
    gtext = jnp.concatenate((gck_low, gpair[:, columns:]), 1)
    text_part = nt(gtext, w_text).astype(BF16)
    text_sub = half // 2
    text_part = text_part[: 2 * half].astype(F32) + hop(
        text_part[2 * half :], hop_w
    ).astype(F32)
    text_part = text_part.reshape(2, 2, text_sub, width)
    text_share = lax.dynamic_index_in_dim(text_part, x, 1, keepdims=False)
    text_given = lax.dynamic_index_in_dim(text_part, 1 - x, 1, keepdims=False)
    text_share = text_share + hop(text_given.astype(BF16), hop_x).astype(F32)
    grad_text = give_back(
        text_share.astype(BF16).reshape(2 * text_sub, width),
        text_sub,
        lambda place_here: ((place_here & 1) << 1) | (place_here >> 1),
    ).astype(F32)

    grad_branch_one_share = (grad_state_one * shift(2)).astype(BF16)
    grad_branch_one = spread(grad_branch_one_share)
    grad_attn = nn(grad_branch_one, w_attn_out).astype(BF16)
    grad_query, grad_key, grad_value = attend_back(
        query_low, grad_attn, key_all, value_all, ids_here, key_code, total_self, True
    )
    kv_back = scatter_tokens(jnp.concatenate((grad_key, grad_value), 1))
    grad_qnorm = rotate(grad_query, cosine, -sine)
    grad_knorm = rotate(kv_back[:, :columns].astype(F32), cosine, -sine)
    sums_self = token_sum(
        jnp.stack(
            (
                jnp.sum(gains[0] * grad_qnorm * query_pre, -1),
                jnp.sum(gains[1] * grad_knorm * key_pre, -1),
            )
        )
    )
    gq_low = rms_back(query_pre, inverse_q, gains[0], grad_qnorm, sums_self[0])
    gk_low = rms_back(key_pre, inverse_k, gains[1], grad_knorm, sums_self[1])
    grad_proj = jnp.concatenate((gq_low, gk_low, kv_back[:, columns:]), 1)
    grad_act = collect(nt(grad_proj, w_attn))
    grad_input_share = grad_state_one + norm_back(state_in, grad_act * (1.0 + shift(1)))

    grad_mid = scatter_weight(
        jnp.concatenate(
            (
                tn(grad_branch_one, attn_low),
                tn(cross_act, gcq_low),
                tn(grad_branch_two, cross_low),
            ),
            1,
        )
    )
    grad_text_in = scatter_weight(tn(text_here, gtext))
    grad_attn_in = scatter_weight(tn(act_low, grad_proj))

    rows_sum = lambda a: jnp.sum(a.astype(F32), 0)
    column_sums = jnp.concatenate(
        (
            rows_sum(grad_proj),
            rows_sum(gcq_low),
            rows_sum(gtext),
            rows_sum(grad_qnorm * query_pre * inverse_q),
            rows_sum(grad_knorm * key_pre * inverse_k),
            rows_sum(grad_cquery * cquery_pre * inverse_cq),
            rows_sum(gckey * ckey_pre * inverse_ck),
            rows_sum(grad_hidden),
        )
    )
    column_sums = all_sum(column_sums, [hop_c] + hop_rest + [hop_k])
    low_sums = column_sums.astype(BF16)
    column_sums = by_home(low_sums, hop(low_sums, hop_w)).astype(F32)
    grad_in_bias = column_sums[: 6 * columns].reshape(2, 3, columns)
    grad_gains = column_sums[6 * columns : 10 * columns].reshape(4, columns)
    grad_ffn_bias = column_sums[10 * columns :]

    picker = (
        ids_share == jnp.arange(latents, dtype=jnp.int32)[None, :]
    ).astype(F32)

    def by_latent(value):
        return lax.dot_general(
            picker, value, (((0,), (0,)), ((), ())), precision=HIGH, preferred_element_type=F32
        )

    feature_sums = jnp.concatenate(
        [
            by_latent(grad_act),
            by_latent(grad_act * normed_one),
            by_latent(grad_state_one * branch_one),
            by_latent(grad_ffn_act),
            by_latent(grad_ffn_act * normed_two),
            by_latent(grad_top * branch_three),
        ]
        + [
            rows_sum(a)[None]
            for a in (
                grad_branch_one_share,
                grad_branch_two_share,
                grad_branch_three_share,
                grad_cross_act * normed_three,
                grad_cross_act,
            )
        ],
        0,
    )
    feature_sums = all_sum(feature_sums, [hop_c, hop_x, hop_w] + hop_rest)
    low_features = feature_sums.astype(BF16)
    far_features = hop(low_features, hop_k).astype(F32)
    near_features = low_features.astype(F32)
    both_sums = near_features + far_features
    count = 6 * latents
    near_temb = near_features[:count].reshape(6, latents, width).transpose(1, 0, 2)
    far_temb = far_features[:count].reshape(6, latents, width).transpose(1, 0, 2)
    grad_temb = jnp.where(
        k == 0, jnp.stack((near_temb, far_temb)), jnp.stack((far_temb, near_temb))
    )
    grad_mod = jnp.sum(grad_temb, (0, 1))

    block_out = give_back(out_share, piece, lambda place_here: place_here)
    grad_inputs = give_back(
        grad_input_share.astype(BF16), piece, lambda place_here: place_here
    ).astype(F32)
    unpack = lambda a: a.reshape(slice_rows, -1, columns).transpose(1, 0, 2).astype(F32)
    return (
        block_out,
        grad_inputs,
        grad_text,
        grad_temb,
        grad_mod,
        unpack(grad_attn_in),
        grad_in_bias,
        grad_gains,
        grad_mid[:, :columns].T.astype(F32),
        jnp.concatenate(
            (grad_mid[None, :, columns : 2 * columns].astype(F32), unpack(grad_text_in)), 0
        ),
        grad_mid[:, 2 * columns :].T.astype(F32),
        both_sums[count + 3],
        both_sums[count + 4],
        grad_up.astype(F32),
        grad_ffn_bias,
        grad_down.T.astype(F32),
        both_sums[count : count + 3],
    )


def solution(mesh):
    placed = (
        P(None, "seq", None),
        P(None, "seq", None),
        P(),
        P(),
        P(None, "seq", "tensor"),
        P(None, None, "tensor"),
        P(None, "tensor"),
        P("tensor", "seq"),
        P(None, "seq", "tensor"),
        P("tensor", "seq"),
        P(),
        P(),
        P("seq", "tensor"),
        P("tensor"),
        P("tensor", "seq"),
        P(),
        P(None, "seq"),
        P(None, "seq"),
        P(None, "seq"),
        P(None, "seq"),
        P(None, "seq"),
        P(None, "seq", None),
    )
    return jax.shard_map(
        shards,
        mesh=mesh,
        in_specs=placed,
        out_specs=(
            P(None, "seq", None),
            P(None, "seq", None),
            P(None, "seq", None),
            P(),
            P(),
            P(None, "seq", "tensor"),
            P(None, None, "tensor"),
            P(None, "tensor"),
            P("tensor", "seq"),
            P(None, "seq", "tensor"),
            P("tensor", "seq"),
            P(),
            P(),
            P("seq", "tensor"),
            P("tensor"),
            P("tensor", "seq"),
            P(),
        ),
        check_vma=False,
    )
```

```python
import math

import jax
import jax.numpy as jnp
from jax import lax
from jax.experimental import pallas as pl
from jax.experimental.layout import Layout, with_layout_constraint
from jax.experimental.pallas import tpu as pltpu
from jax.sharding import PartitionSpec as P

HD = 128
TXT = 512
EPS = 1e-06
NEG = -1e30
F32 = jnp.float32
BF16 = jnp.bfloat16
AXES = ("seq", "tensor")
SCALE = 1.0 / math.sqrt(HD)
SCALE_TWO = SCALE * math.log2(math.e)
STEP = 32


def nn(a, b):
    return lax.dot_general(a, b, (((1,), (0,)), ((), ())), preferred_element_type=F32)


def nt(a, b):
    return lax.dot_general(a, b, (((1,), (1,)), ((), ())), preferred_element_type=F32)


def tn(a, b):
    return lax.dot_general(a, b, (((0,), (0,)), ((), ())), preferred_element_type=F32)


def shape_of(rows, cols, kind=F32):
    return jax.ShapeDtypeStruct((rows, cols), kind)


def padded_bytes(array):
    size = jnp.dtype(array.dtype).itemsize
    rows, cols = array.shape[-2:]
    return -(-rows // (32 // size)) * (32 // size) * -(-cols // HD) * HD * size


def vmem_call(kernel, outs, args, name, scratch=(), room=2):
    whole = pl.BlockSpec(memory_space=pltpu.VMEM)
    held = sum(padded_bytes(a) for a in (*outs, *args, *scratch))
    return pl.pallas_call(
        kernel,
        out_shape=outs,
        in_specs=[whole] * len(args),
        out_specs=[whole] * len(outs),
        scratch_shapes=list(scratch),
        cost_estimate=pl.CostEstimate(flops=1024, bytes_accessed=1024, transcendentals=0),
        compiler_params=pltpu.CompilerParams(
            vmem_limit_bytes=min(held + room * 2**20, 60 * 2**20)
        ),
        name=name,
    )(*args)


def by_rows(rows, step, body):
    def one(i, carry):
        body(pl.ds(pl.multiple_of(i * step, step), step))
        return carry

    lax.fori_loop(0, rows // step, one, 0)


def center_of(values):
    center = values - jnp.mean(values, -1, keepdims=True)
    return center, lax.rsqrt(jnp.mean(center * center, -1, keepdims=True) + EPS)


def pull_norm(center, inverse, cotangent):
    normed = center * inverse
    return inverse * (
        cotangent
        - jnp.mean(cotangent, -1, keepdims=True)
        - normed * jnp.mean(cotangent * normed, -1, keepdims=True)
    )


def chooser(vec_ref, ids, latents):
    def choose(number):
        out = vec_ref[number : number + 1, :]
        for latent in range(1, latents):
            row = latent * 6 + number
            out = jnp.where(ids == latent, vec_ref[row : row + 1, :], out)
        return out

    return choose


def add_latents(sums_ref, first, ids, value, latents):
    for latent in range(latents):
        row = first + latent
        part = jnp.sum(jnp.where(ids == latent, value, 0.0), 0, keepdims=True)
        sums_ref[row : row + 1, :] += part


def add_row(sums_ref, row, value):
    sums_ref[row : row + 1, :] += jnp.sum(value.astype(F32), 0, keepdims=True)


def share_kernels(latents):
    base = 6 * latents

    def three(refs, rows):
        return sum(ref[rows, :].astype(F32) for ref in refs)

    def first(state_ref, grad_ref, ids_ref, vec_ref, act_ref, top_ref):
        def body(rows):
            choose = chooser(vec_ref, ids_ref[rows, :], latents)
            center, inverse = center_of(state_ref[rows, :].astype(F32))
            act_ref[rows, :] = (
                center * inverse * (1.0 + choose(1)) + choose(0)
            ).astype(BF16)
            top_ref[rows, :] = (grad_ref[rows, :].astype(F32) * choose(5)).astype(BF16)

        by_rows(state_ref.shape[0], STEP, body)

    def middle(p0, p1, p2, state_ref, ids_ref, vec_ref, next_ref, branch_ref, act_ref):
        def body(rows):
            choose = chooser(vec_ref, ids_ref[rows, :], latents)
            branch = three((p0, p1, p2), rows) + vec_ref[base : base + 1, :]
            state = state_ref[rows, :].astype(F32) + branch * choose(2)
            branch_ref[rows, :] = branch
            next_ref[rows, :] = state
            center, inverse = center_of(state)
            act_ref[rows, :] = (
                center * inverse * vec_ref[base + 3 : base + 4, :]
                + vec_ref[base + 4 : base + 5, :]
            ).astype(BF16)

        by_rows(state_ref.shape[0], STEP, body)

    def last(p0, p1, p2, state_ref, ids_ref, vec_ref, next_ref, act_ref):
        def body(rows):
            choose = chooser(vec_ref, ids_ref[rows, :], latents)
            branch = three((p0, p1, p2), rows) + vec_ref[base + 1 : base + 2, :]
            state = state_ref[rows, :] + branch
            next_ref[rows, :] = state
            center, inverse = center_of(state)
            act_ref[rows, :] = (
                center * inverse * (1.0 + choose(4)) + choose(3)
            ).astype(BF16)

        by_rows(state_ref.shape[0], STEP, body)

    def result(p0, p1, p2, state_ref, grad_ref, ids_ref, vec_ref, out_ref, sums_ref):
        sums_ref[...] = jnp.zeros_like(sums_ref)

        def body(rows):
            ids = ids_ref[rows, :]
            choose = chooser(vec_ref, ids, latents)
            branch = three((p0, p1, p2), rows) + vec_ref[base + 2 : base + 3, :]
            out_ref[rows, :] = (state_ref[rows, :] + branch * choose(5)).astype(BF16)
            grad = grad_ref[rows, :].astype(F32)
            add_latents(sums_ref, 0, ids, grad * branch, latents)

        by_rows(state_ref.shape[0], STEP, body)

    def back_last(
        p0, p1, p2, state_ref, grad_ref, top_ref, ids_ref, vec_ref, next_ref, low_ref, sums_ref
    ):
        sums_ref[...] = jnp.zeros_like(sums_ref)

        def body(rows):
            ids = ids_ref[rows, :]
            choose = chooser(vec_ref, ids, latents)
            grad_act = three((p0, p1, p2), rows)
            center, inverse = center_of(state_ref[rows, :])
            grad = grad_ref[rows, :].astype(F32) + pull_norm(
                center, inverse, grad_act * (1.0 + choose(4))
            )
            next_ref[rows, :] = grad
            low = grad.astype(BF16)
            low_ref[rows, :] = low
            add_latents(sums_ref, 0, ids, grad_act, latents)
            add_latents(sums_ref, latents, ids, grad_act * center * inverse, latents)
            add_row(sums_ref, 2 * latents, low)
            add_row(sums_ref, 2 * latents + 1, top_ref[rows, :])

        by_rows(state_ref.shape[0], STEP, body)

    def back_middle(
        p0,
        p1,
        p2,
        state_ref,
        grad_ref,
        branch_ref,
        ids_ref,
        vec_ref,
        next_ref,
        low_ref,
        sums_ref,
    ):
        sums_ref[...] = jnp.zeros_like(sums_ref)

        def body(rows):
            ids = ids_ref[rows, :]
            choose = chooser(vec_ref, ids, latents)
            grad_act = three((p0, p1, p2), rows)
            center, inverse = center_of(state_ref[rows, :])
            grad = grad_ref[rows, :] + pull_norm(
                center, inverse, grad_act * vec_ref[base + 3 : base + 4, :]
            )
            next_ref[rows, :] = grad
            low = (grad * choose(2)).astype(BF16)
            low_ref[rows, :] = low
            add_latents(sums_ref, 0, ids, grad * branch_ref[rows, :], latents)
            add_row(sums_ref, latents, low)
            add_row(sums_ref, latents + 1, grad_act * center * inverse)
            add_row(sums_ref, latents + 2, grad_act)

        by_rows(state_ref.shape[0], STEP, body)

    def back_first(p0, p1, p2, state_ref, grad_ref, ids_ref, vec_ref, out_ref, sums_ref):
        sums_ref[...] = jnp.zeros_like(sums_ref)

        def body(rows):
            ids = ids_ref[rows, :]
            choose = chooser(vec_ref, ids, latents)
            grad_act = three((p0, p1, p2), rows)
            center, inverse = center_of(state_ref[rows, :].astype(F32))
            out_ref[rows, :] = (
                grad_ref[rows, :] + pull_norm(center, inverse, grad_act * (1.0 + choose(1)))
            ).astype(BF16)
            add_latents(sums_ref, 0, ids, grad_act, latents)
            add_latents(sums_ref, latents, ids, grad_act * center * inverse, latents)

        by_rows(state_ref.shape[0], STEP, body)

    return first, middle, last, result, back_last, back_middle, back_first


def join_kernel(*refs):
    start = 0
    for ref in refs[:-1]:
        rows = ref.shape[0]
        refs[-1][start : start + rows, :] = ref[...]
        start += rows


def join(pieces):
    rows, cols = sum(p.shape[0] for p in pieces), pieces[0].shape[1]
    return vmem_call(join_kernel, [shape_of(rows, cols, BF16)], pieces, "join")[0]


def fold_kernel(to_x, to_w, from_x, from_w, out_x, out_w):
    half = from_x.shape[0]
    add = lambda a, b: (a.astype(F32) + b.astype(F32)).astype(BF16)
    out_x[:half, :] = to_x[:half, :]
    out_x[half:, :] = add(to_x[half:, :], from_w[...])
    out_w[:half, :] = add(to_w[:half, :], from_x[...])
    out_w[half:, :] = to_w[half:, :]


def project_out(values, weight, first, count):
    rows, width = values.shape[0], weight.shape[0]
    share = rows // 4
    heights = (share, share, share, share // 2, share // 2)
    tile = 256 if width % 256 == 0 else width

    def kernel(value_ref, weight_ref, *outs):
        for n in range(width // tile):
            cols = slice(n * tile, (n + 1) * tile)
            part = nt(value_ref[...], weight_ref[cols, first : first + count]).astype(BF16)
            start = 0
            for out in outs:
                out[:, cols] = part[start : start + out.shape[0], :]
                start += out.shape[0]

    return vmem_call(
        kernel, [shape_of(h, width, BF16) for h in heights], (values, weight), "project_out"
    )


def put_lines(out_ref, columns):
    rows = columns[0].shape[0]
    lane = lax.broadcasted_iota(jnp.int32, (rows, HD), 1)
    flat = jnp.zeros((rows, HD), F32)
    for i, column in enumerate(columns):
        flat = jnp.where(lane == i, column, flat)
    out_ref[...] = flat.T[:8, :]


def take_lines(refs):
    rows = refs[0].shape[1]
    share = rows // 4
    total = refs[0][...]
    for j in (1, 2, 3):
        total = total + jnp.concatenate(
            [refs[j][:, (i ^ j) * share : ((i ^ j) + 1) * share] for i in range(4)], 1
        )
    return jnp.concatenate([total] * (HD // 8), 0).T


def squares(values, columns, count):
    rows = values.shape[0]

    def kernel(value_ref, out_ref):
        parts = []
        for i in range(count):
            part = value_ref[:, i * columns : (i + 1) * columns]
            parts.append(jnp.sum(part * part, -1, keepdims=True))
        put_lines(out_ref, parts)

    return vmem_call(kernel, [shape_of(8, rows)], (values,), "squares")[0]


def turn(values, cosine, signed):
    even = lax.broadcasted_iota(jnp.int32, values.shape, 1) % 2 == 0
    other = jnp.where(even, pltpu.roll(values, HD - 1, 1), pltpu.roll(values, 1, 1))
    return values * cosine + other * signed


def shape_heads(projected, lines, gains, cosine, signed, width):
    rows = projected.shape[0]
    columns = gains.shape[1]

    def kernel(value_ref, l0, l1, l2, l3, gain_ref, cos_ref, sin_ref, query_ref, pair_ref, inv_ref):
        inv_ref[...] = lax.rsqrt(take_lines((l0, l1, l2, l3)) / width + EPS)

        def body(here):
            cos, sin = cos_ref[here, :], sin_ref[here, :]
            for head in range(columns // HD):
                for i, ref in ((0, query_ref), (1, pair_ref)):
                    at = i * columns + head * HD
                    cols = slice(head * HD, (head + 1) * HD)
                    value = (
                        value_ref[here, at : at + HD]
                        * inv_ref[here, i : i + 1]
                        * gain_ref[i : i + 1, cols]
                    )
                    ref[here, cols] = turn(value, cos, sin).astype(BF16)
            pair_ref[here, columns:] = value_ref[here, 2 * columns :].astype(BF16)

        by_rows(rows, STEP, body)

    return vmem_call(
        kernel,
        [shape_of(rows, columns, BF16), shape_of(rows, 2 * columns, BF16), shape_of(rows, HD)],
        (projected, *lines, gains, cosine, signed),
        "shape_heads",
    )


def shape_cross(projected, lines, gains, width):
    rows, columns = projected.shape

    def kernel(value_ref, l0, l1, l2, l3, gain_ref, query_ref, inv_ref):
        inv_ref[...] = lax.rsqrt(take_lines((l0, l1, l2, l3)) / width + EPS)

        def body(here):
            query_ref[here, :] = (
                value_ref[here, :] * inv_ref[here, 0:1] * gain_ref[2:3, :]
            ).astype(BF16)

        by_rows(rows, STEP, body)

    return vmem_call(
        kernel,
        [shape_of(rows, columns, BF16), shape_of(rows, HD)],
        (projected, *lines, gains),
        "shape_cross",
    )


def turn_back(dquery, pair, projected, gains, cosine, signed):
    rows, columns = dquery.shape

    def kernel(dq_ref, pair_ref, value_ref, gain_ref, cos_ref, sin_ref, gq_ref, gk_ref, line_ref, sum_ref):
        lane = lax.broadcasted_iota(jnp.int32, (STEP, HD), 1)

        def body(here):
            cos, sin = cos_ref[here, :], -sin_ref[here, :]
            totals = []
            for i, ref, out in ((0, dq_ref, gq_ref), (1, pair_ref, gk_ref)):
                total = jnp.zeros((STEP, 1), F32)
                for head in range(columns // HD):
                    cols = slice(head * HD, (head + 1) * HD)
                    at = i * columns + head * HD
                    back = turn(ref[here, cols].astype(F32), cos, sin)
                    out[here, cols] = back
                    total = total + jnp.sum(
                        gain_ref[i : i + 1, cols] * back * value_ref[here, at : at + HD],
                        -1,
                        keepdims=True,
                    )
                totals.append(total)
            sum_ref[here, :] = jnp.where(
                lane == 0, totals[0], jnp.where(lane == 1, totals[1], 0.0)
            )

        by_rows(rows, STEP, body)
        line_ref[...] = sum_ref[...].T[:8, :]

    return vmem_call(
        kernel,
        [shape_of(rows, columns), shape_of(rows, columns), shape_of(8, rows)],
        (dquery, pair, projected, gains, cosine, signed),
        "turn_back",
        [pltpu.VMEM((rows, HD), F32)],
    )


def rms_pull(pre, inverse, gain, cotangent, summed, width):
    scaled = inverse * inverse * inverse * summed / width
    return (inverse * gain * cotangent - pre * scaled).astype(BF16)


def back_heads(gquery, gkey, projected, inverse, pair, lines, gains, width):
    rows, columns = gquery.shape

    def kernel(gq_ref, gk_ref, value_ref, inv_ref, pair_ref, l0, l1, l2, l3, gain_ref, out_ref, sums_ref, sum_ref):
        sum_ref[...] = take_lines((l0, l1, l2, l3))
        sums_ref[...] = jnp.zeros_like(sums_ref)

        def body(here):
            for i, ref in ((0, gq_ref), (1, gk_ref)):
                cols = slice(i * columns, (i + 1) * columns)
                pre, grad, inv = value_ref[here, cols], ref[here, :], inv_ref[here, i : i + 1]
                low = rms_pull(pre, inv, gain_ref[i : i + 1, :], grad, sum_ref[here, i : i + 1], width)
                out_ref[here, cols] = low
                sums_ref[0:1, cols] += jnp.sum(low.astype(F32), 0, keepdims=True)
                sums_ref[1:2, cols] += jnp.sum(grad * pre * inv, 0, keepdims=True)
            cols = slice(2 * columns, 3 * columns)
            value = pair_ref[here, columns:]
            out_ref[here, cols] = value
            sums_ref[0:1, cols] += jnp.sum(value.astype(F32), 0, keepdims=True)

        by_rows(rows, STEP, body)

    return vmem_call(
        kernel,
        [shape_of(rows, 3 * columns, BF16), shape_of(8, 3 * columns)],
        (gquery, gkey, projected, inverse, pair, *lines, gains),
        "back_heads",
        [pltpu.VMEM((rows, HD), F32)],
    )


def cross_lines(dquery, pre, gains):
    rows = dquery.shape[0]

    def kernel(dq_ref, pre_ref, gain_ref, line_ref):
        put_lines(
            line_ref,
            [jnp.sum(gain_ref[2:3, :] * dq_ref[...] * pre_ref[...], -1, keepdims=True)],
        )

    return vmem_call(kernel, [shape_of(8, rows)], (dquery, pre, gains), "cross_lines")[0]


def back_cross(dquery, pre, inverse, lines, gains, width):
    rows, columns = dquery.shape

    def kernel(dq_ref, pre_ref, inv_ref, l0, l1, l2, l3, gain_ref, out_ref, sums_ref, sum_ref):
        sum_ref[...] = take_lines((l0, l1, l2, l3))
        sums_ref[...] = jnp.zeros_like(sums_ref)

        def body(here):
            grad, before, inv = dq_ref[here, :], pre_ref[here, :], inv_ref[here, 0:1]
            low = rms_pull(before, inv, gain_ref[2:3, :], grad, sum_ref[here, 0:1], width)
            out_ref[here, :] = low
            sums_ref[0:1, :] += jnp.sum(low.astype(F32), 0, keepdims=True)
            sums_ref[1:2, :] += jnp.sum(grad * before * inv, 0, keepdims=True)

        by_rows(rows, STEP, body)

    return vmem_call(
        kernel,
        [shape_of(rows, columns, BF16), shape_of(8, columns)],
        (dquery, pre, inverse, *lines, gains),
        "back_cross",
        [pltpu.VMEM((rows, HD), F32)],
    )


def own_pairs(same, first, diagonal):
    if not (diagonal and first):
        return same
    row = lax.broadcasted_iota(jnp.int32, same.shape, 0)
    col = lax.broadcasted_iota(jnp.int32, same.shape, 1)
    return same | (row == col)


def attend(queries, pairs, query_code, key_code, diagonal):
    rows, width = queries.shape
    height = pairs[0].shape[0]
    count = height * len(pairs)

    def kernel(query_ref, qcode_ref, kcode_ref, *refs):
        piece_refs = refs[: len(pairs)]
        out_ref, low_ref, line_ref, score_ref = refs[len(pairs) :]
        code = qcode_ref[...]
        totals = []
        for head in range(width // HD):
            cols = slice(head * HD, (head + 1) * HD)
            query = query_ref[:, cols]
            top = None
            for i, ref in enumerate(piece_refs):
                here = slice(i * height, (i + 1) * height)
                same = own_pairs(code == kcode_ref[:, here], i == 0, diagonal)
                scores = jnp.where(same, nt(query, ref[:, cols]), NEG)
                score_ref[:, here] = scores
                peak = jnp.max(scores, -1, keepdims=True)
                top = peak if top is None else jnp.maximum(top, peak)
            out = None
            total = None
            for i, ref in enumerate(piece_refs):
                here = slice(i * height, (i + 1) * height)
                weights = jnp.exp2((score_ref[:, here] - top) * SCALE_TWO)
                score_ref[:, here] = weights
                part = jnp.sum(weights, -1, keepdims=True)
                total = part if total is None else total + part
            inverse = 1.0 / total
            for i, ref in enumerate(piece_refs):
                here = slice(i * height, (i + 1) * height)
                probs = (score_ref[:, here] * inverse).astype(BF16)
                at = width + head * HD
                part = nn(probs, ref[:, at : at + HD])
                out = part if out is None else out + part
            out_ref[:, cols] = out
            low_ref[:, cols] = out.astype(BF16)
            totals.append(top * SCALE_TWO + jnp.log2(total))
        put_lines(line_ref, totals)

    return vmem_call(
        kernel,
        [shape_of(rows, width), shape_of(rows, width, BF16), shape_of(8, rows)],
        (queries, query_code[:, None], key_code[None, :], *pairs),
        "attend" if diagonal else "attend_text",
        [pltpu.VMEM((rows, count), F32)],
        2 * len(pairs),
    )


def attend_back(queries, grads, full, lines, pairs, query_code, key_code, diagonal):
    rows, width = queries.shape
    height = pairs[0].shape[0]
    number = len(pairs)

    def kernel(query_ref, grad_ref, full_ref, line_ref, qcode_ref, kcode_ref, *refs):
        piece_refs = refs[:number]
        dquery_ref, near_ref, far_ref = refs[number:]
        heads = width // HD
        lane = lax.broadcasted_iota(jnp.int32, (rows, HD), 1)
        flat = jnp.zeros((rows, HD), F32)
        for head in range(heads):
            cols = slice(head * HD, (head + 1) * HD)
            delta = jnp.sum(grad_ref[:, cols].astype(F32) * full_ref[:, cols], -1, keepdims=True)
            flat = jnp.where(lane == head, delta, flat)
        deltas = flat.T
        code = qcode_ref[...]
        for head in range(heads):
            cols = slice(head * HD, (head + 1) * HD)
            query, grad = query_ref[:, cols], grad_ref[:, cols]
            dquery = None
            for i, ref in enumerate(piece_refs):
                here = slice(i * height, (i + 1) * height)
                key, value = ref[:, cols], ref[:, width + head * HD : width + (head + 1) * HD]
                same = own_pairs(kcode_ref[here, :] == code, i == 0, diagonal)
                weights = jnp.exp2(nt(key, query) * SCALE_TWO - line_ref[head : head + 1, :])
                probs = jnp.where(same, weights, 0.0)
                dscores = (probs * (nt(value, grad) - deltas[head : head + 1, :])).astype(BF16)
                out, start = (near_ref, i) if 2 * i < number else (far_ref, i - number // 2)
                spot = slice(start * height, (start + 1) * height)
                out[spot, cols] = (nn(dscores, query) * SCALE).astype(BF16)
                out[spot, width + head * HD : width + (head + 1) * HD] = nn(
                    probs.astype(BF16), grad
                ).astype(BF16)
                part = tn(dscores, key)
                dquery = part if dquery is None else dquery + part
            dquery_ref[:, cols] = dquery * SCALE

    half = shape_of(height * number // 2, 2 * width, BF16)
    return vmem_call(
        kernel,
        [shape_of(rows, width), half, half],
        (queries, grads, full, lines, query_code[None, :], key_code[:, None], *pairs),
        "attend_back" if diagonal else "attend_text_back",
        (),
        2 * number,
    )


def rope_tables(frames, rows_pos, cols_pos):
    part_size = HD // 6
    widths = (HD - 4 * part_size, 2 * part_size, 2 * part_size)
    rates, picks = [], []
    for i, group_width in enumerate(widths):
        exponent = jnp.arange(0, group_width, 2).astype(F32) / group_width
        rates.append(jnp.repeat(jnp.power(10000.0, -exponent), 2))
        picks.append(jnp.full((group_width,), i, jnp.int32))
    rate, pick = jnp.concatenate(rates)[None], jnp.concatenate(picks)[None]
    places = [p.astype(F32)[:, None] for p in (frames, rows_pos, cols_pos)]
    angle = jnp.where(pick == 0, places[0], jnp.where(pick == 1, places[1], places[2])) * rate
    sign = jnp.where(jnp.arange(HD) % 2 == 0, -1.0, 1.0).astype(F32)
    return jnp.cos(angle), jnp.sin(angle) * sign[None]


def shards(
    inputs,
    text_states,
    timestep_emb,
    modulation,
    attn_in,
    in_bias,
    norm_gains,
    attn_out,
    cross_in,
    cross_out,
    cross_norm_gain,
    cross_norm_bias,
    ffn_in,
    ffn_bias,
    ffn_out,
    out_bias,
    latent_ids,
    pad_mask,
    frame_pos,
    row_pos,
    col_pos,
    cotangent,
):
    micros, tok_rows, width = inputs.shape
    text_rows = text_states.shape[1]
    latents = timestep_emb.shape[1]
    columns = attn_in.shape[2]
    hidden = ffn_in.shape[1]
    slice_rows = attn_in.shape[1]
    seq_size, tensor_size = lax.axis_size("seq"), lax.axis_size("tensor")
    places = seq_size * tensor_size
    bits = seq_size.bit_length() - 1
    s, t = lax.axis_index("seq"), lax.axis_index("tensor")
    top = bits - 1
    rest = [b for b in range(bits) if b not in (1, top)]

    def seq_bit(b):
        return (s >> b) & 1

    k, w, x, c = seq_bit(top), seq_bit(1), t >> 1, t & 1
    own_slice = (s & ~2) | (c << 1)
    hop_c, hop_x, hop_w, hop_k = 1, 2, tensor_size << 1, tensor_size << top
    hop_rest = [tensor_size << b for b in rest]
    hop_group = [0, hop_x, hop_w, hop_x | hop_w]

    def hop(value, mask):
        return lax.ppermute(value, AXES, [(d, d ^ mask) for d in range(places)])

    def swap(value):
        def other(d):
            low, high = d & 1, (d // hop_w) & 1
            return d if low == high else d ^ 1 ^ hop_w

        return lax.ppermute(value, AXES, [(d, other(d)) for d in range(places)])

    def swap_far(value):
        def other(d):
            low, high = d & 1, (d // hop_w) & 1
            return (d if low == high else d ^ 1 ^ hop_w) ^ hop_k

        return lax.ppermute(value, AXES, [(d, other(d)) for d in range(places)])

    near_masks = [hop_c] + hop_rest[::-1]
    near_groups = []
    taken = set()
    for d in range(places):
        if d not in taken:
            members = [d]
            for mask in near_masks[::-1]:
                members = members + [m ^ mask for m in members]
            taken |= set(members)
            near_groups.append(members)

    far_groups = []
    for members in near_groups:
        if not members[0] & hop_k:
            far_groups.append([m ^ mask for m in members for mask in (0, hop_k)])

    def by_k(own, far):
        return jnp.where(k == 0, jnp.stack((own, far)), jnp.stack((far, own)))

    def place_weight(block):
        return by_k(swap(block), swap_far(block))

    def gather_weight(placed):
        out = lax.all_gather(
            placed, AXES, axis=0, tiled=False, axis_index_groups=near_groups
        )
        return out.reshape(seq_size * slice_rows, -1)

    def gather_far(block):
        out = lax.all_gather(
            block, AXES, axis=0, tiled=False, axis_index_groups=far_groups
        )
        return out.reshape(seq_size * slice_rows, -1)

    def scatter_weight(grad):
        return lax.psum_scatter(
            grad,
            AXES,
            scatter_dimension=0,
            tiled=True,
            axis_index_groups=near_groups,
        ).reshape(2, slice_rows, grad.shape[1])

    def home_parts(parts):
        own = lax.dynamic_index_in_dim(parts, k, 0, keepdims=False)
        far = lax.dynamic_index_in_dim(parts, 1 - k, 0, keepdims=False)
        return swap(own), swap_far(far)

    def whole_of(home):
        return home[0].astype(F32) + home[1].astype(F32)

    def weight_grad(a, b):
        return with_layout_constraint(tn(a, b).astype(BF16), Layout((0, 1)))

    def slice_at(place):
        number = (place & 1) << top
        place >>= 1
        for bit_number in rest:
            number |= (place & 1) << bit_number
            place >>= 1
        return number | (place << 1)

    order = [slice_at(place) for place in range(seq_size)]
    order_back = [order.index(i) for i in range(seq_size)]

    def arrange(value, order_here):
        return jnp.concatenate(
            [value[..., i * slice_rows : (i + 1) * slice_rows] for i in order_here], -1
        )

    def tie(*values):
        return lax.optimization_barrier(values)

    def after(value, *anchors):
        return tie(value, *anchors)[0]

    def gather_pieces(value):
        pieces = [value]
        for mask in hop_rest + [hop_c]:
            pieces = pieces + [hop(p, mask) for p in pieces]
        return pieces

    def add_low(a, b):
        return (a.astype(F32) + b.astype(F32)).astype(BF16)

    def spread(value, beside=(), later=()):
        half = value.shape[0] // 2
        by_x, by_w = hop(value, hop_x), hop(value, hop_w)
        if beside:
            by_x, by_w, beside = tie(by_x, by_w, beside)
        far = (hop(by_w[:half], hop_x), hop(by_x[half:], hop_w))
        if later:
            far, later = tie(far, later)
        whole = join((value, by_x, by_w) + far)
        return (whole, *beside, *later) if beside or later else whole

    def collect(values, weight, first, count, beside=(), later=()):
        own, to_x, to_w, far_x, far_w = project_out(values, weight, first, count)
        from_x, from_w = hop(far_x, hop_x), hop(far_w, hop_w)
        if beside:
            from_x, from_w, beside = tie(from_x, from_w, beside)
        kinds = [shape_of(*to_x.shape, BF16)] * 2
        to_x, to_w = vmem_call(fold_kernel, kinds, (to_x, to_w, from_x, from_w), "fold")
        got_x, got_w = hop(to_x, hop_x), hop(to_w, hop_w)
        if later:
            got_x, got_w, later = tie(got_x, got_w, later)
        return ((own, got_x, got_w), *beside, *later)

    def lines_of(value):
        return (value,) + tuple(hop(value, m) for m in hop_group[1:])

    def text_sum(value):
        total = value
        half_rows = value.shape[-1] // 2
        for j in (1, 2, 3):
            other = hop(value, hop_group[j])
            if j > 1:
                other = jnp.concatenate((other[..., half_rows:], other[..., :half_rows]), -1)
            total = total + other
        return total

    def all_sum(value, masks):
        for mask in masks:
            value = value.astype(BF16)
            value = value.astype(F32) + hop(value, mask).astype(F32)
        return value

    def by_home(own, other):
        return jnp.where(c == w, own, other)

    piece = tok_rows // 4
    group_rows = 8 * piece
    share_rows = 2 * piece

    def take_share(array):
        parts = array.reshape(micros, 4, piece, width)
        pick = lambda micro: arrange(
            lax.dynamic_index_in_dim(
                lax.dynamic_index_in_dim(parts, micro, 0, keepdims=False), t, 0, keepdims=False
            ),
            order,
        )
        return jnp.concatenate((pick(k), hop(pick(1 - k), hop_k)), 0)

    def give_far(share):
        rows_each = share.shape[0] // 2
        share = arrange(share, order_back)
        own, far = share[:rows_each], hop(share[rows_each:], hop_k)
        return jnp.where(k == 0, jnp.stack((own, far)), jnp.stack((far, own)))

    def give_across(both):
        return both, hop(both, hop_x)

    def give_back(both, across, position):
        rows_each = both.shape[1]
        pieces = ((0, both), (1, hop(both, hop_c)), (2, across), (3, hop(across, hop_c)))
        out = jnp.zeros((micros, 4, rows_each, width), both.dtype)
        for offset, value in pieces:
            out = lax.dynamic_update_index_in_dim(out, value, position(t ^ offset), 1)
        return out.reshape(micros, 4 * rows_each, width)

    meta = jnp.stack((latent_ids, pad_mask, frame_pos, row_pos, col_pos))[None]
    for mask in [hop_k, hop_w] + hop_rest:
        meta = jnp.concatenate((meta, hop(meta, mask)), 0)
    meta = lax.dynamic_index_in_dim(meta, k, 2, keepdims=False)
    meta = meta.reshape((2,) * bits + (5, 2, 2, piece))
    meta = jnp.where(x == 1, jnp.flip(meta, bits + 1), meta)
    meta = jnp.where(c == 1, jnp.flip(meta, bits + 2), meta)
    others = list(range(bits - 2))
    meta = meta.transpose([bits, bits + 2] + others + [bits - 2, bits + 1, bits - 1, bits + 3])
    meta = meta.reshape(5, -1)
    ids_all = meta[0]
    key_code = jnp.where(meta[1] == 1, ids_all, -1)
    ids_here = ids_all[:group_rows]
    ids_share = ids_here[:share_rows, None]
    cosine, signed = rope_tables(*(meta[i, :group_rows] for i in (2, 3, 4)))

    state_in = take_share(inputs)
    table = modulation + lax.dynamic_index_in_dim(timestep_emb, k, 0, keepdims=False)
    vectors = arrange(
        jnp.concatenate(
            (
                table.reshape(latents * 6, width),
                out_bias.astype(F32),
                cross_norm_gain[None].astype(F32),
                cross_norm_bias[None].astype(F32),
            ),
            0,
        ),
        order,
    )

    pack = lambda a: a.transpose(1, 0, 2).reshape(slice_rows, -1)
    placed_attn = place_weight(pack(attn_in))
    grad_top = take_share(cotangent)
    (
        share_first,
        share_middle,
        share_last,
        share_result,
        share_back_last,
        share_back_middle,
        share_back_first,
    ) = share_kernels(latents)
    share_low = shape_of(share_rows, width, BF16)
    share_full = shape_of(share_rows, width)
    sums_shape = lambda count: shape_of(count, width)
    act_share, top_share = vmem_call(
        share_first,
        [share_low, share_low],
        (state_in, grad_top, ids_share, vectors),
        "share_first",
    )
    act_low = spread(act_share)
    w_attn = gather_weight(after(placed_attn, act_low))
    mid_block = jnp.concatenate((pack(cross_in[1:]), attn_out.T, cross_in[0], cross_out.T), 1)
    placed_mid = place_weight(after(mid_block, placed_attn))

    flat = jnp.concatenate((in_bias.reshape(-1), norm_gains.reshape(-1), ffn_bias))
    flat = by_home(flat, hop(flat, hop_c)).astype(F32)
    bias_in = flat[: 6 * columns].reshape(2, 3, columns)
    gains = flat[6 * columns : 10 * columns].reshape(4, columns)
    bias_ffn = flat[10 * columns :]

    half = text_rows // 2
    texts = text_states.reshape(micros, 2, half, width)

    def text_of(micro):
        own = lax.dynamic_index_in_dim(
            lax.dynamic_index_in_dim(texts, micro, 0, keepdims=False), c, 0, keepdims=False
        )
        return arrange(own, order)

    text_here = jnp.concatenate((text_of(k), hop(text_of(1 - k), hop_k)), 0)
    text_here = jnp.concatenate((text_here, hop(text_here, hop_w)), 0)
    number = jnp.arange(4 * half * seq_size // 2, dtype=jnp.int32)
    row, chunk = number % half, number // half
    row_k, row_w, row_rest = chunk & 1, (chunk >> 1) & 1, chunk >> 2
    place = ((row_k ^ k) << top) | ((row_w ^ w) << 1)
    for i, b in enumerate(rest):
        place = place | ((((row_rest >> i) & 1) ^ seq_bit(b)) << b)
    row_c = (row_rest >> len(rest)) ^ c
    text_code = (place * text_rows + row_c * half + row) // TXT

    act_low, placed_mid, text_here = tie(act_low, placed_mid, text_here)
    projected = nn(act_low, w_attn) + bias_in[0].reshape(1, -1)
    w_mid = gather_weight(after(placed_mid, projected))
    lines = lines_of(squares(projected, columns, 2))
    swapped_up = swap(after(ffn_in, projected))
    query_low, pair, inverse = shape_heads(projected, lines, gains, cosine, signed, width)
    pairs = gather_pieces(pair)
    pairs, swapped_up = tie(pairs, swapped_up)
    w_up = gather_far(swapped_up)
    attn_full, attn_low, attn_lines = attend(query_low, pairs, ids_here, key_code, True)
    down_block = after(ffn_out.T, query_low)
    hidden_half = hidden // 2
    down_parts = [down_block[:, :hidden_half], down_block[:, hidden_half:]]
    placed_down = [place_weight(down_parts[0])]
    text_pre = nn(text_here, w_mid[:, : 2 * columns]) + bias_in[1, 1:].reshape(1, -1)
    parts, text_pre, placed_first = collect(
        attn_low, w_mid, 2 * columns, columns, (text_pre,), (placed_down[0],)
    )
    state_one, branch_one, cross_share = vmem_call(
        share_middle,
        [share_full, share_full, share_low],
        (*parts, state_in, ids_share, vectors),
        "share_middle",
    )

    ckey_pre = text_pre[:, :columns]
    inverse_ck = lax.rsqrt(
        text_sum(jnp.sum(ckey_pre * ckey_pre, -1)[None])[0] / width + EPS
    )[:, None]
    text_pair = jnp.concatenate(
        (
            (ckey_pre * inverse_ck * gains[3]).astype(BF16),
            text_pre[:, columns:].astype(BF16),
        ),
        1,
    )

    cross_act, text_pair = spread(cross_share, (text_pair,))
    text_pairs = gather_pieces(text_pair)
    placed_second = place_weight(after(down_parts[1], placed_first))
    cquery_pre = nn(cross_act, w_mid[:, 3 * columns : 4 * columns]) + bias_in[1, 0]
    cross_lines_here = lines_of(squares(cquery_pre, columns, 1))
    cross_lines_here, text_pairs = tie(cross_lines_here, text_pairs)
    cquery_low, inverse_cq = shape_cross(cquery_pre, cross_lines_here, gains, width)
    cross_full, cross_low, total_lines = attend(
        cquery_low, text_pairs, ids_here, text_code, False
    )
    parts, placed_second = collect(
        cross_low, w_mid, 4 * columns, columns, (), (placed_second,)
    )
    w_down = gather_weight(jnp.concatenate((placed_first, placed_second), 2))
    state_two, ffn_share = vmem_call(
        share_last,
        [share_full, share_low],
        (*parts, state_one, ids_share, vectors),
        "share_last",
    )

    ffn_act = spread(ffn_share)
    hidden_pre = nn(ffn_act, w_up) + bias_ffn
    hidden_low = jax.nn.gelu(hidden_pre, approximate=True).astype(BF16)
    grad_branch_three = spread(after(top_share, cross_act))

    gelu_pull = jax.vjp(lambda h: jax.nn.gelu(h, approximate=True), hidden_pre)[1]
    grad_hidden = gelu_pull(nn(grad_branch_three, w_down))[0].astype(BF16)
    part_down = weight_grad(grad_branch_three, hidden_low)
    part_up = weight_grad(ffn_act, grad_hidden)
    half_down = scatter_weight(part_down)
    half_up = scatter_weight(part_up)
    parts, part_down, part_up = collect(
        grad_hidden, w_up, 0, hidden, (part_down,), (part_up,)
    )
    grad_two, gb2_share, sums_two = vmem_call(
        share_back_last,
        [share_full, share_low, sums_shape(2 * latents + 2)],
        (*parts, state_two, grad_top, top_share, ids_share, vectors),
        "share_back_last",
    )

    grad_branch_two = spread(gb2_share)
    out_parts, = collect(after(hidden_low, gb2_share), w_down, 0, hidden)
    out_share, sums_three = vmem_call(
        share_result,
        [share_low, sums_shape(latents)],
        (*out_parts, state_two, grad_top, ids_share, vectors),
        "share_result",
    )
    grad_cross = nn(grad_branch_two, w_mid[:, 4 * columns :]).astype(BF16)
    grad_cquery, text_near, text_far = attend_back(
        cquery_low,
        grad_cross,
        cross_full,
        total_lines,
        text_pairs,
        ids_here,
        text_code,
        False,
    )
    back_lines = lines_of(cross_lines(grad_cquery, cquery_pre, gains))
    text_far = hop(text_far, hop_c)
    back_lines, text_far = tie(back_lines, text_far)
    gcq_low, sums_cq = back_cross(
        grad_cquery, cquery_pre, inverse_cq, back_lines, gains, width
    )
    gpair = add_low(text_near, text_far)
    for mask in hop_rest[::-1]:
        rows_left = gpair.shape[0] // 2
        gpair = add_low(gpair[:rows_left], hop(gpair[rows_left:], mask))
    parts, gpair, out_share = collect(
        gcq_low, w_mid, 3 * columns, columns, (), (gpair, out_share)
    )
    grad_one, gb1_share, sums_one = vmem_call(
        share_back_middle,
        [share_full, share_low, sums_shape(latents + 3)],
        (*parts, state_one, grad_two, branch_one, ids_share, vectors),
        "share_back_middle",
    )

    gckey = gpair[:, :columns].astype(F32)
    sums_ck = text_sum(jnp.sum(gains[3] * gckey * ckey_pre, -1)[None])[0]
    out_both = give_far(out_share)
    grad_branch_one, sums_ck, out_both = spread(gb1_share, (sums_ck,), (out_both,))
    out_both, out_across = give_across(out_both)
    gck_low = rms_pull(ckey_pre, inverse_ck, gains[3], gckey, sums_ck[:, None], width)
    gtext = jnp.concatenate((gck_low, gpair[:, columns:]), 1)
    text_part = nt(gtext, w_mid[:, : 2 * columns]).astype(BF16)
    text_back = hop(text_part[2 * half :], hop_w)

    grad_attn = nn(grad_branch_one, w_mid[:, 2 * columns : 3 * columns]).astype(BF16)
    part_mid = jnp.concatenate(
        (
            weight_grad(text_here, gtext),
            weight_grad(grad_branch_one, attn_low),
            weight_grad(cross_act, gcq_low),
            weight_grad(grad_branch_two, cross_low),
        ),
        1,
    )
    half_mid = scatter_weight(part_mid)
    grad_attn, text_back, out_across = tie(grad_attn, text_back, out_across)
    block_out = give_back(out_both, out_across, lambda place_here: place_here)
    grad_query, near, far = attend_back(
        query_low, grad_attn, attn_full, attn_lines, pairs, ids_here, key_code, True
    )
    text_sub = half // 2
    text_part = text_part[: 2 * half].astype(F32) + text_back.astype(F32)
    text_part = text_part.reshape(2, 2, text_sub, width)
    text_share = lax.dynamic_index_in_dim(text_part, x, 1, keepdims=False)
    text_given = lax.dynamic_index_in_dim(text_part, 1 - x, 1, keepdims=False)
    text_got = hop(text_given.astype(BF16), hop_x)
    far = hop(far, hop_c)
    far, text_got = tie(far, text_got)
    kv_back = add_low(near, far)
    text_share = (text_share + text_got.astype(F32)).astype(BF16)
    text_both = give_far(text_share.reshape(2 * text_sub, width))
    home_down = [home_parts(half_down[:, :, :hidden_half])]
    for mask in hop_rest[::-1]:
        rows_left = kv_back.shape[0] // 2
        given = hop(kv_back[rows_left:], mask)
        if mask == hop_rest[0]:
            given, text_both, home_down[0] = tie(given, text_both, home_down[0])
        kv_back = add_low(kv_back[:rows_left], given)
    text_both, text_across = give_across(text_both)
    gquery, gkey, head_lines = turn_back(
        grad_query, kv_back, projected, gains, cosine, signed
    )
    head_lines = lines_of(head_lines)
    head_lines, text_across, block_out = tie(head_lines, text_across, block_out)
    grad_proj, sums_heads = back_heads(
        gquery, gkey, projected, inverse, kv_back, head_lines, gains, width
    )
    grad_text = give_back(
        text_both,
        text_across,
        lambda place_here: ((place_here & 1) << 1) | (place_here >> 1),
    ).astype(F32)
    part_attn = weight_grad(act_low, grad_proj)
    part_attn = part_attn.reshape((2,) * (bits - 1) + (2, slice_rows, 3 * columns))
    steps = [(0, hop_c, c)] + [
        (1 + i, tensor_size << b, seq_bit(b)) for i, b in enumerate(rest[::-1])
    ]
    for axis, mask, mine in steps:
        kept = lax.dynamic_index_in_dim(part_attn, mine, axis, keepdims=True)
        given = lax.dynamic_index_in_dim(part_attn, 1 - mine, axis, keepdims=True)
        part_attn = add_low(kept, hop(given, mask))
    part_attn = part_attn.reshape(2, slice_rows, 3 * columns)
    home_down.append(home_parts(after(half_down[:, :, hidden_half:], home_down[0])))
    home_up = [home_parts(half_up[:, :, :hidden_half])]
    parts, home_down[1], home_up[0] = collect(
        grad_proj, w_attn, 0, 3 * columns, (home_down[1],), (home_up[0],)
    )
    grad_share, sums_zero = vmem_call(
        share_back_first,
        [share_low, sums_shape(2 * latents)],
        (*parts, state_in, grad_one, ids_share, vectors),
        "share_back_first",
    )
    home_up.append(home_parts(after(half_up[:, :, hidden_half:], home_up[0])))
    in_both = give_far(grad_share)
    in_both, home_up[1] = tie(in_both, home_up[1])
    in_both, in_across = give_across(in_both)
    home_mid = home_parts(half_mid)
    in_across, home_mid = tie(in_across, home_mid)
    grad_inputs = give_back(in_both, in_across, lambda place_here: place_here).astype(F32)
    grad_attn_in = whole_of(home_parts(part_attn))
    grad_mid = whole_of(home_mid)
    grad_up = jnp.concatenate([whole_of(h) for h in home_up], 1)
    grad_down = jnp.concatenate([whole_of(h) for h in home_down], 1)

    rows_sum = lambda a: jnp.sum(a.astype(F32), 0)
    extra = -hidden % columns
    column_sums = jnp.concatenate(
        (
            sums_heads[0].reshape(3, columns),
            sums_cq[:1],
            rows_sum(gtext).reshape(2, columns),
            sums_heads[1, : 2 * columns].reshape(2, columns),
            sums_cq[1:2],
            rows_sum(gckey * ckey_pre * inverse_ck)[None],
            jnp.pad(rows_sum(grad_hidden), (0, extra)).reshape(-1, columns),
        ),
        0,
    )
    column_sums = all_sum(column_sums, [hop_c] + hop_rest + [hop_k])
    low_sums = column_sums.astype(BF16)
    column_sums = by_home(low_sums, hop(low_sums, hop_w)).astype(F32)
    grad_in_bias = column_sums[:6].reshape(2, 3, columns)
    grad_gains = column_sums[6:10]
    grad_ffn_bias = column_sums[10:].reshape(-1)[:hidden]

    count = latents
    feature_sums = jnp.concatenate(
        (
            sums_zero,
            sums_one[:count],
            sums_two[: 2 * count],
            sums_three,
            sums_one[count : count + 1],
            sums_two[2 * count :],
            sums_one[count + 1 :],
        ),
        0,
    )
    feature_sums = all_sum(feature_sums, [hop_c, hop_x, hop_w] + hop_rest)
    low_features = arrange(feature_sums.astype(BF16), order_back)
    far_features = hop(low_features, hop_k).astype(F32)
    near_features = low_features.astype(F32)
    both_sums = near_features + far_features
    count = 6 * latents
    near_temb = near_features[:count].reshape(6, latents, width).transpose(1, 0, 2)
    far_temb = far_features[:count].reshape(6, latents, width).transpose(1, 0, 2)
    grad_temb = jnp.where(
        k == 0, jnp.stack((near_temb, far_temb)), jnp.stack((far_temb, near_temb))
    )
    grad_mod = jnp.sum(grad_temb, (0, 1))

    unpack = lambda a: a.reshape(slice_rows, -1, columns).transpose(1, 0, 2)
    part = lambda i: grad_mid[:, i * columns : (i + 1) * columns]
    return (
        block_out,
        grad_inputs,
        grad_text,
        grad_temb,
        grad_mod,
        unpack(grad_attn_in),
        grad_in_bias,
        grad_gains,
        part(2).T,
        jnp.stack((part(3), part(0), part(1))),
        part(4).T,
        both_sums[count + 3],
        both_sums[count + 4],
        grad_up,
        grad_ffn_bias,
        grad_down.T,
        both_sums[count : count + 3],
    )


def solution(mesh):
    placed = (
        P(None, "seq", None),
        P(None, "seq", None),
        P(),
        P(),
        P(None, "seq", "tensor"),
        P(None, None, "tensor"),
        P(None, "tensor"),
        P("tensor", "seq"),
        P(None, "seq", "tensor"),
        P("tensor", "seq"),
        P(),
        P(),
        P("seq", "tensor"),
        P("tensor"),
        P("tensor", "seq"),
        P(),
        P(None, "seq"),
        P(None, "seq"),
        P(None, "seq"),
        P(None, "seq"),
        P(None, "seq"),
        P(None, "seq", None),
    )
    return jax.shard_map(
        shards,
        mesh=mesh,
        in_specs=placed,
        out_specs=(
            P(None, "seq", None),
            P(None, "seq", None),
            P(None, "seq", None),
            P(),
            P(),
            P(None, "seq", "tensor"),
            P(None, None, "tensor"),
            P(None, "tensor"),
            P("tensor", "seq"),
            P(None, "seq", "tensor"),
            P("tensor", "seq"),
            P(),
            P(),
            P("seq", "tensor"),
            P("tensor"),
            P("tensor", "seq"),
            P(),
        ),
        check_vma=False,
    )
```

```python
import math

import jax
import jax.numpy as jnp
from jax import lax
from jax.experimental import pallas as pl
from jax.experimental.layout import Layout, with_layout_constraint
from jax.experimental.pallas import tpu as pltpu
from jax.sharding import PartitionSpec as P

HD = 128
TXT = 512
EPS = 1e-06
NEG = -1e30
F32 = jnp.float32
BF16 = jnp.bfloat16
AXES = ("seq", "tensor")
SCALE = 1.0 / math.sqrt(HD)
SCALE_TWO = SCALE * math.log2(math.e)
STEP = 32
HEAD_STEP = 128


def nn(a, b):
    return lax.dot_general(a, b, (((1,), (0,)), ((), ())), preferred_element_type=F32)


def nt(a, b):
    return lax.dot_general(a, b, (((1,), (1,)), ((), ())), preferred_element_type=F32)


def tn(a, b):
    return lax.dot_general(a, b, (((0,), (0,)), ((), ())), preferred_element_type=F32)


def shape_of(rows, cols, kind=F32):
    return jax.ShapeDtypeStruct((rows, cols), kind)


def padded_bytes(array):
    size = jnp.dtype(array.dtype).itemsize
    rows, cols = array.shape[-2:]
    return -(-rows // (32 // size)) * (32 // size) * -(-cols // HD) * HD * size


def vmem_call(kernel, outs, args, name, scratch=(), room=2):
    whole = pl.BlockSpec(memory_space=pltpu.VMEM)
    held = sum(padded_bytes(a) for a in (*outs, *args, *scratch))
    return pl.pallas_call(
        kernel,
        out_shape=outs,
        in_specs=[whole] * len(args),
        out_specs=[whole] * len(outs),
        scratch_shapes=list(scratch),
        cost_estimate=pl.CostEstimate(flops=1024, bytes_accessed=1024, transcendentals=0),
        compiler_params=pltpu.CompilerParams(
            vmem_limit_bytes=min(held + room * 2**20, 60 * 2**20)
        ),
        name=name,
    )(*args)


def by_rows(rows, step, body):
    def one(i, carry):
        body(pl.ds(pl.multiple_of(i * step, step), step))
        return carry

    lax.fori_loop(0, rows // step, one, 0)


def center_of(values):
    center = values - jnp.mean(values, -1, keepdims=True)
    return center, lax.rsqrt(jnp.mean(center * center, -1, keepdims=True) + EPS)


def pull_norm(center, inverse, cotangent):
    normed = center * inverse
    return inverse * (
        cotangent
        - jnp.mean(cotangent, -1, keepdims=True)
        - normed * jnp.mean(cotangent * normed, -1, keepdims=True)
    )


def chooser(vec_ref, ids, latents):
    def choose(number):
        out = vec_ref[number : number + 1, :]
        for latent in range(1, latents):
            row = latent * 6 + number
            out = jnp.where(ids == latent, vec_ref[row : row + 1, :], out)
        return out

    return choose


def add_latents(sums_ref, first, ids, value, latents):
    for latent in range(latents):
        row = first + latent
        part = jnp.sum(jnp.where(ids == latent, value, 0.0), 0, keepdims=True)
        sums_ref[row : row + 1, :] += part


def add_row(sums_ref, row, value):
    sums_ref[row : row + 1, :] += jnp.sum(value.astype(F32), 0, keepdims=True)


def share_kernels(latents):
    base = 6 * latents

    def three(refs, rows):
        return sum(ref[rows, :].astype(F32) for ref in refs)

    def first(state_ref, ids_ref, vec_ref, act_ref):
        def body(rows):
            choose = chooser(vec_ref, ids_ref[rows, :], latents)
            center, inverse = center_of(state_ref[rows, :].astype(F32))
            act_ref[rows, :] = (
                center * inverse * (1.0 + choose(1)) + choose(0)
            ).astype(BF16)

        by_rows(state_ref.shape[0], STEP, body)

    def top(grad_ref, ids_ref, vec_ref, top_ref):
        def body(rows):
            choose = chooser(vec_ref, ids_ref[rows, :], latents)
            top_ref[rows, :] = (grad_ref[rows, :].astype(F32) * choose(5)).astype(BF16)

        by_rows(grad_ref.shape[0], STEP, body)

    def middle(p0, p1, p2, state_ref, ids_ref, vec_ref, next_ref, branch_ref, act_ref):
        def body(rows):
            choose = chooser(vec_ref, ids_ref[rows, :], latents)
            branch = three((p0, p1, p2), rows) + vec_ref[base : base + 1, :]
            state = state_ref[rows, :].astype(F32) + branch * choose(2)
            branch_ref[rows, :] = branch
            next_ref[rows, :] = state
            center, inverse = center_of(state)
            act_ref[rows, :] = (
                center * inverse * vec_ref[base + 3 : base + 4, :]
                + vec_ref[base + 4 : base + 5, :]
            ).astype(BF16)

        by_rows(state_ref.shape[0], STEP, body)

    def last(p0, p1, p2, state_ref, ids_ref, vec_ref, next_ref, act_ref):
        def body(rows):
            choose = chooser(vec_ref, ids_ref[rows, :], latents)
            branch = three((p0, p1, p2), rows) + vec_ref[base + 1 : base + 2, :]
            state = state_ref[rows, :] + branch
            next_ref[rows, :] = state
            center, inverse = center_of(state)
            act_ref[rows, :] = (
                center * inverse * (1.0 + choose(4)) + choose(3)
            ).astype(BF16)

        by_rows(state_ref.shape[0], STEP, body)

    def result(p0, p1, p2, state_ref, grad_ref, ids_ref, vec_ref, out_ref, sums_ref):
        sums_ref[...] = jnp.zeros_like(sums_ref)

        def body(rows):
            ids = ids_ref[rows, :]
            choose = chooser(vec_ref, ids, latents)
            branch = three((p0, p1, p2), rows) + vec_ref[base + 2 : base + 3, :]
            out_ref[rows, :] = (state_ref[rows, :] + branch * choose(5)).astype(BF16)
            grad = grad_ref[rows, :].astype(F32)
            add_latents(sums_ref, 0, ids, grad * branch, latents)

        by_rows(state_ref.shape[0], STEP, body)

    def back_last(
        p0, p1, p2, state_ref, grad_ref, top_ref, ids_ref, vec_ref, next_ref, low_ref, sums_ref
    ):
        sums_ref[...] = jnp.zeros_like(sums_ref)

        def body(rows):
            ids = ids_ref[rows, :]
            choose = chooser(vec_ref, ids, latents)
            grad_act = three((p0, p1, p2), rows)
            center, inverse = center_of(state_ref[rows, :])
            grad = grad_ref[rows, :].astype(F32) + pull_norm(
                center, inverse, grad_act * (1.0 + choose(4))
            )
            next_ref[rows, :] = grad
            low = grad.astype(BF16)
            low_ref[rows, :] = low
            add_latents(sums_ref, 0, ids, grad_act, latents)
            add_latents(sums_ref, latents, ids, grad_act * center * inverse, latents)
            add_row(sums_ref, 2 * latents, low)
            add_row(sums_ref, 2 * latents + 1, top_ref[rows, :])

        by_rows(state_ref.shape[0], STEP, body)

    def back_middle(
        p0,
        p1,
        p2,
        state_ref,
        grad_ref,
        branch_ref,
        ids_ref,
        vec_ref,
        next_ref,
        low_ref,
        sums_ref,
    ):
        sums_ref[...] = jnp.zeros_like(sums_ref)

        def body(rows):
            ids = ids_ref[rows, :]
            choose = chooser(vec_ref, ids, latents)
            grad_act = three((p0, p1, p2), rows)
            center, inverse = center_of(state_ref[rows, :])
            grad = grad_ref[rows, :] + pull_norm(
                center, inverse, grad_act * vec_ref[base + 3 : base + 4, :]
            )
            next_ref[rows, :] = grad
            low = (grad * choose(2)).astype(BF16)
            low_ref[rows, :] = low
            add_latents(sums_ref, 0, ids, grad * branch_ref[rows, :], latents)
            add_row(sums_ref, latents, low)
            add_row(sums_ref, latents + 1, grad_act * center * inverse)
            add_row(sums_ref, latents + 2, grad_act)

        by_rows(state_ref.shape[0], STEP, body)

    def back_first(p0, p1, p2, state_ref, grad_ref, ids_ref, vec_ref, out_ref, sums_ref):
        sums_ref[...] = jnp.zeros_like(sums_ref)

        def body(rows):
            ids = ids_ref[rows, :]
            choose = chooser(vec_ref, ids, latents)
            grad_act = three((p0, p1, p2), rows)
            center, inverse = center_of(state_ref[rows, :].astype(F32))
            out_ref[rows, :] = (
                grad_ref[rows, :] + pull_norm(center, inverse, grad_act * (1.0 + choose(1)))
            ).astype(BF16)
            add_latents(sums_ref, 0, ids, grad_act, latents)
            add_latents(sums_ref, latents, ids, grad_act * center * inverse, latents)

        by_rows(state_ref.shape[0], STEP, body)

    return first, top, middle, last, result, back_last, back_middle, back_first


def join_kernel(*refs):
    start = 0
    for ref in refs[:-1]:
        rows = ref.shape[0]
        refs[-1][start : start + rows, :] = ref[...]
        start += rows


def join(pieces):
    rows, cols = sum(p.shape[0] for p in pieces), pieces[0].shape[1]
    return vmem_call(join_kernel, [shape_of(rows, cols, BF16)], pieces, "join")[0]


def fold_kernel(to_x, to_w, from_x, from_w, out_x, out_w):
    half = from_x.shape[0]
    add = lambda a, b: (a.astype(F32) + b.astype(F32)).astype(BF16)
    out_x[:half, :] = to_x[:half, :]
    out_x[half:, :] = add(to_x[half:, :], from_w[...])
    out_w[:half, :] = add(to_w[:half, :], from_x[...])
    out_w[half:, :] = to_w[half:, :]


def project_out(values, weight, first, count):
    rows, width = values.shape[0], weight.shape[0]
    share = rows // 4
    heights = (share, share, share, share // 2, share // 2)
    tile = 256 if width % 256 == 0 else width

    def kernel(value_ref, weight_ref, *outs):
        for n in range(width // tile):
            cols = slice(n * tile, (n + 1) * tile)
            part = nt(value_ref[...], weight_ref[cols, first : first + count]).astype(BF16)
            start = 0
            for out in outs:
                out[:, cols] = part[start : start + out.shape[0], :]
                start += out.shape[0]

    return vmem_call(
        kernel, [shape_of(h, width, BF16) for h in heights], (values, weight), "project_out"
    )


def put_lines(out_ref, columns):
    rows = columns[0].shape[0]
    lane = lax.broadcasted_iota(jnp.int32, (rows, HD), 1)
    flat = jnp.zeros((rows, HD), F32)
    for i, column in enumerate(columns):
        flat = jnp.where(lane == i, column, flat)
    out_ref[...] = flat.T[:8, :]


def take_lines(refs):
    rows = refs[0].shape[1]
    share = rows // 4
    total = refs[0][...]
    for j in (1, 2, 3):
        total = total + jnp.concatenate(
            [refs[j][:, (i ^ j) * share : ((i ^ j) + 1) * share] for i in range(4)], 1
        )
    return jnp.concatenate([total] * (HD // 8), 0).T


def squares(values, columns, count, text=None):
    rows = values.shape[0]
    args = (values,) if text is None else (values, text)

    def kernel(*refs):
        out_ref = refs[-1]
        parts = []
        for i in range(count):
            part = refs[0][:, i * columns : (i + 1) * columns]
            parts.append(jnp.sum(part * part, -1, keepdims=True))
        if text is not None:
            part = refs[1][:, :columns]
            total = jnp.sum(part * part, -1, keepdims=True)
            rest = jnp.zeros((rows - part.shape[0], 1), F32)
            parts.append(jnp.concatenate((total, rest), 0))
        put_lines(out_ref, parts)

    return vmem_call(kernel, [shape_of(8, rows)], args, "squares")[0]


def turn(values, cosine, signed):
    even = lax.broadcasted_iota(jnp.int32, values.shape, 1) % 2 == 0
    other = jnp.where(even, pltpu.roll(values, HD - 1, 1), pltpu.roll(values, 1, 1))
    return values * cosine + other * signed


def shape_heads(projected, lines, gains, cosine, signed, width):
    rows = projected.shape[0]
    columns = gains.shape[1]

    def kernel(value_ref, l0, l1, l2, l3, gain_ref, cos_ref, sin_ref, query_ref, pair_ref, inv_ref):
        inv_ref[...] = lax.rsqrt(take_lines((l0, l1, l2, l3)) / width + EPS)

        def body(here):
            cos, sin = cos_ref[here, :], sin_ref[here, :]
            for head in range(columns // HD):
                for i, ref in ((0, query_ref), (1, pair_ref)):
                    at = i * columns + head * HD
                    cols = slice(head * HD, (head + 1) * HD)
                    value = (
                        value_ref[here, at : at + HD]
                        * inv_ref[here, i : i + 1]
                        * gain_ref[i : i + 1, cols]
                    )
                    ref[here, cols] = turn(value, cos, sin).astype(BF16)
            pair_ref[here, columns:] = value_ref[here, 2 * columns :].astype(BF16)

        by_rows(rows, HEAD_STEP, body)

    return vmem_call(
        kernel,
        [shape_of(rows, columns, BF16), shape_of(rows, 2 * columns, BF16), shape_of(rows, HD)],
        (projected, *lines, gains, cosine, signed),
        "shape_heads",
    )


def shape_cross(projected, lines, gains, width):
    rows, columns = projected.shape

    def kernel(value_ref, l0, l1, l2, l3, gain_ref, query_ref, inv_ref):
        inv_ref[...] = lax.rsqrt(take_lines((l0, l1, l2, l3)) / width + EPS)

        def body(here):
            query_ref[here, :] = (
                value_ref[here, :] * inv_ref[here, 0:1] * gain_ref[2:3, :]
            ).astype(BF16)

        by_rows(rows, HEAD_STEP, body)

    return vmem_call(
        kernel,
        [shape_of(rows, columns, BF16), shape_of(rows, HD)],
        (projected, *lines, gains),
        "shape_cross",
    )


def turn_back(dquery, pair, projected, gains, cosine, signed):
    rows, columns = dquery.shape

    def kernel(dq_ref, pair_ref, value_ref, gain_ref, cos_ref, sin_ref, gq_ref, gk_ref, line_ref, sum_ref):
        lane = lax.broadcasted_iota(jnp.int32, (HEAD_STEP, HD), 1)

        def body(here):
            cos, sin = cos_ref[here, :], -sin_ref[here, :]
            totals = []
            for i, ref, out in ((0, dq_ref, gq_ref), (1, pair_ref, gk_ref)):
                total = jnp.zeros((HEAD_STEP, 1), F32)
                for head in range(columns // HD):
                    cols = slice(head * HD, (head + 1) * HD)
                    at = i * columns + head * HD
                    back = turn(ref[here, cols].astype(F32), cos, sin)
                    out[here, cols] = back
                    total = total + jnp.sum(
                        gain_ref[i : i + 1, cols] * back * value_ref[here, at : at + HD],
                        -1,
                        keepdims=True,
                    )
                totals.append(total)
            sum_ref[here, :] = jnp.where(
                lane == 0, totals[0], jnp.where(lane == 1, totals[1], 0.0)
            )

        by_rows(rows, HEAD_STEP, body)
        line_ref[...] = sum_ref[...].T[:8, :]

    return vmem_call(
        kernel,
        [shape_of(rows, columns), shape_of(rows, columns), shape_of(8, rows)],
        (dquery, pair, projected, gains, cosine, signed),
        "turn_back",
        [pltpu.VMEM((rows, HD), F32)],
    )


def rms_pull(pre, inverse, gain, cotangent, summed, width):
    scaled = inverse * inverse * inverse * summed / width
    return (inverse * gain * cotangent - pre * scaled).astype(BF16)


def back_heads(gquery, gkey, projected, inverse, pair, lines, gains, width):
    rows, columns = gquery.shape

    def kernel(gq_ref, gk_ref, value_ref, inv_ref, pair_ref, l0, l1, l2, l3, gain_ref, out_ref, sums_ref, sum_ref):
        sum_ref[...] = take_lines((l0, l1, l2, l3))
        sums_ref[...] = jnp.zeros_like(sums_ref)

        def body(here):
            for i, ref in ((0, gq_ref), (1, gk_ref)):
                cols = slice(i * columns, (i + 1) * columns)
                pre, grad, inv = value_ref[here, cols], ref[here, :], inv_ref[here, i : i + 1]
                low = rms_pull(pre, inv, gain_ref[i : i + 1, :], grad, sum_ref[here, i : i + 1], width)
                out_ref[here, cols] = low
                sums_ref[0:1, cols] += jnp.sum(low.astype(F32), 0, keepdims=True)
                sums_ref[1:2, cols] += jnp.sum(grad * pre * inv, 0, keepdims=True)
            cols = slice(2 * columns, 3 * columns)
            value = pair_ref[here, columns:]
            out_ref[here, cols] = value
            sums_ref[0:1, cols] += jnp.sum(value.astype(F32), 0, keepdims=True)

        by_rows(rows, HEAD_STEP, body)

    return vmem_call(
        kernel,
        [shape_of(rows, 3 * columns, BF16), shape_of(8, 3 * columns)],
        (gquery, gkey, projected, inverse, pair, *lines, gains),
        "back_heads",
        [pltpu.VMEM((rows, HD), F32)],
    )


def cross_lines(dquery, pre, gains):
    rows = dquery.shape[0]

    def kernel(dq_ref, pre_ref, gain_ref, line_ref):
        put_lines(
            line_ref,
            [jnp.sum(gain_ref[2:3, :] * dq_ref[...] * pre_ref[...], -1, keepdims=True)],
        )

    return vmem_call(kernel, [shape_of(8, rows)], (dquery, pre, gains), "cross_lines")[0]


def back_cross(dquery, pre, inverse, lines, gains, width):
    rows, columns = dquery.shape

    def kernel(dq_ref, pre_ref, inv_ref, l0, l1, l2, l3, gain_ref, out_ref, sums_ref, sum_ref):
        sum_ref[...] = take_lines((l0, l1, l2, l3))
        sums_ref[...] = jnp.zeros_like(sums_ref)

        def body(here):
            grad, before, inv = dq_ref[here, :], pre_ref[here, :], inv_ref[here, 0:1]
            low = rms_pull(before, inv, gain_ref[2:3, :], grad, sum_ref[here, 0:1], width)
            out_ref[here, :] = low
            sums_ref[0:1, :] += jnp.sum(low.astype(F32), 0, keepdims=True)
            sums_ref[1:2, :] += jnp.sum(grad * before * inv, 0, keepdims=True)

        by_rows(rows, HEAD_STEP, body)

    return vmem_call(
        kernel,
        [shape_of(rows, columns, BF16), shape_of(8, columns)],
        (dquery, pre, inverse, *lines, gains),
        "back_cross",
        [pltpu.VMEM((rows, HD), F32)],
    )


def own_pairs(same, first, diagonal):
    if not (diagonal and first):
        return same
    row = lax.broadcasted_iota(jnp.int32, same.shape, 0)
    col = lax.broadcasted_iota(jnp.int32, same.shape, 1)
    return same | (row == col)


def attend(queries, pairs, query_code, key_code, diagonal):
    rows, width = queries.shape
    height = pairs[0].shape[0]
    count = height * len(pairs)

    def kernel(query_ref, qcode_ref, kcode_ref, *refs):
        piece_refs = refs[: len(pairs)]
        out_ref, low_ref, line_ref, score_ref = refs[len(pairs) :]
        code = qcode_ref[...]
        totals = []
        for head in range(width // HD):
            cols = slice(head * HD, (head + 1) * HD)
            query = query_ref[:, cols]
            top = None
            for i, ref in enumerate(piece_refs):
                here = slice(i * height, (i + 1) * height)
                same = own_pairs(code == kcode_ref[:, here], i == 0, diagonal)
                scores = jnp.where(same, nt(query, ref[:, cols]), NEG)
                score_ref[:, here] = scores
                peak = jnp.max(scores, -1, keepdims=True)
                top = peak if top is None else jnp.maximum(top, peak)
            out = None
            total = None
            for i, ref in enumerate(piece_refs):
                here = slice(i * height, (i + 1) * height)
                weights = jnp.exp2((score_ref[:, here] - top) * SCALE_TWO)
                score_ref[:, here] = weights
                part = jnp.sum(weights, -1, keepdims=True)
                total = part if total is None else total + part
            inverse = 1.0 / total
            for i, ref in enumerate(piece_refs):
                here = slice(i * height, (i + 1) * height)
                probs = (score_ref[:, here] * inverse).astype(BF16)
                at = width + head * HD
                part = nn(probs, ref[:, at : at + HD])
                out = part if out is None else out + part
            out_ref[:, cols] = out
            low_ref[:, cols] = out.astype(BF16)
            totals.append(top * SCALE_TWO + jnp.log2(total))
        put_lines(line_ref, totals)

    return vmem_call(
        kernel,
        [shape_of(rows, width), shape_of(rows, width, BF16), shape_of(8, rows)],
        (queries, query_code[:, None], key_code[None, :], *pairs),
        "attend" if diagonal else "attend_text",
        [pltpu.VMEM((rows, count), F32)],
        2 * len(pairs),
    )


def attend_back(queries, grads, full, lines, pairs, query_code, key_code, diagonal):
    rows, width = queries.shape
    height = pairs[0].shape[0]
    number = len(pairs)

    def kernel(query_ref, grad_ref, full_ref, line_ref, qcode_ref, kcode_ref, *refs):
        piece_refs = refs[:number]
        dquery_ref, near_ref, far_ref = refs[number:]
        heads = width // HD
        lane = lax.broadcasted_iota(jnp.int32, (rows, HD), 1)
        flat = jnp.zeros((rows, HD), F32)
        for head in range(heads):
            cols = slice(head * HD, (head + 1) * HD)
            delta = jnp.sum(grad_ref[:, cols].astype(F32) * full_ref[:, cols], -1, keepdims=True)
            flat = jnp.where(lane == head, delta, flat)
        deltas = flat.T
        code = qcode_ref[...]
        for head in range(heads):
            cols = slice(head * HD, (head + 1) * HD)
            query, grad = query_ref[:, cols], grad_ref[:, cols]
            dquery = None
            for i, ref in enumerate(piece_refs):
                here = slice(i * height, (i + 1) * height)
                key, value = ref[:, cols], ref[:, width + head * HD : width + (head + 1) * HD]
                same = own_pairs(kcode_ref[here, :] == code, i == 0, diagonal)
                weights = jnp.exp2(nt(key, query) * SCALE_TWO - line_ref[head : head + 1, :])
                probs = jnp.where(same, weights, 0.0)
                dscores = (probs * (nt(value, grad) - deltas[head : head + 1, :])).astype(BF16)
                out, start = (near_ref, i) if 2 * i < number else (far_ref, i - number // 2)
                spot = slice(start * height, (start + 1) * height)
                out[spot, cols] = (nn(dscores, query) * SCALE).astype(BF16)
                out[spot, width + head * HD : width + (head + 1) * HD] = nn(
                    probs.astype(BF16), grad
                ).astype(BF16)
                part = tn(dscores, key)
                dquery = part if dquery is None else dquery + part
            dquery_ref[:, cols] = dquery * SCALE

    half = shape_of(height * number // 2, 2 * width, BF16)
    return vmem_call(
        kernel,
        [shape_of(rows, width), half, half],
        (queries, grads, full, lines, query_code[None, :], key_code[:, None], *pairs),
        "attend_back" if diagonal else "attend_text_back",
        (),
        2 * number,
    )


def rope_tables(frames, rows_pos, cols_pos):
    part_size = HD // 6
    widths = (HD - 4 * part_size, 2 * part_size, 2 * part_size)
    rates, picks = [], []
    for i, group_width in enumerate(widths):
        exponent = jnp.arange(0, group_width, 2).astype(F32) / group_width
        rates.append(jnp.repeat(jnp.power(10000.0, -exponent), 2))
        picks.append(jnp.full((group_width,), i, jnp.int32))
    rate, pick = jnp.concatenate(rates)[None], jnp.concatenate(picks)[None]
    places = [p.astype(F32)[:, None] for p in (frames, rows_pos, cols_pos)]
    angle = jnp.where(pick == 0, places[0], jnp.where(pick == 1, places[1], places[2])) * rate
    sign = jnp.where(jnp.arange(HD) % 2 == 0, -1.0, 1.0).astype(F32)
    return jnp.cos(angle), jnp.sin(angle) * sign[None]


def shards(
    inputs,
    text_states,
    timestep_emb,
    modulation,
    attn_in,
    in_bias,
    norm_gains,
    attn_out,
    cross_in,
    cross_out,
    cross_norm_gain,
    cross_norm_bias,
    ffn_in,
    ffn_bias,
    ffn_out,
    out_bias,
    latent_ids,
    pad_mask,
    frame_pos,
    row_pos,
    col_pos,
    cotangent,
):
    micros, tok_rows, width = inputs.shape
    text_rows = text_states.shape[1]
    latents = timestep_emb.shape[1]
    columns = attn_in.shape[2]
    hidden = ffn_in.shape[1]
    slice_rows = attn_in.shape[1]
    seq_size, tensor_size = lax.axis_size("seq"), lax.axis_size("tensor")
    places = seq_size * tensor_size
    bits = seq_size.bit_length() - 1
    s, t = lax.axis_index("seq"), lax.axis_index("tensor")
    top = bits - 1
    rest = [b for b in range(bits) if b not in (1, top)]

    def seq_bit(b):
        return (s >> b) & 1

    k, w, x, c = seq_bit(top), seq_bit(1), t >> 1, t & 1
    own_slice = (s & ~2) | (c << 1)
    hop_c, hop_x, hop_w, hop_k = 1, 2, tensor_size << 1, tensor_size << top
    hop_rest = [tensor_size << b for b in rest]
    hop_group = [0, hop_x, hop_w, hop_x | hop_w]

    def hop(value, mask):
        return lax.ppermute(value, AXES, [(d, d ^ mask) for d in range(places)])

    def swap(value):
        pairs_here = [
            (d, d ^ 1 ^ hop_w) for d in range(places) if (d & 1) != (d // hop_w) & 1
        ]
        return jnp.where(c == w, value, lax.ppermute(value, AXES, pairs_here))

    def swap_far(value):
        def other(d):
            low, high = d & 1, (d // hop_w) & 1
            return (d if low == high else d ^ 1 ^ hop_w) ^ hop_k

        return lax.ppermute(value, AXES, [(d, other(d)) for d in range(places)])

    near_masks = [hop_c] + hop_rest[::-1]
    near_groups = []
    taken = set()
    for d in range(places):
        if d not in taken:
            members = [d]
            for mask in near_masks[::-1]:
                members = members + [m ^ mask for m in members]
            taken |= set(members)
            near_groups.append(members)

    far_groups = []
    for members in near_groups:
        if not members[0] & hop_k:
            far_groups.append([m ^ mask for m in members for mask in (0, hop_k)])

    def by_k(own, far):
        return jnp.where(k == 0, jnp.stack((own, far)), jnp.stack((far, own)))

    def place_weight(block):
        return by_k(swap(block), swap_far(block))

    def gather_weight(placed):
        out = lax.all_gather(
            placed, AXES, axis=0, tiled=False, axis_index_groups=near_groups
        )
        return out.reshape(seq_size * slice_rows, -1)

    def gather_far(block):
        out = lax.all_gather(
            block, AXES, axis=0, tiled=False, axis_index_groups=far_groups
        )
        return out.reshape(seq_size * slice_rows, -1)

    def scatter_weight(grad):
        return lax.psum_scatter(
            grad,
            AXES,
            scatter_dimension=0,
            tiled=True,
            axis_index_groups=near_groups,
        ).reshape(2, slice_rows, grad.shape[1])

    def scatter_far(grad):
        return lax.psum_scatter(
            grad, AXES, scatter_dimension=0, tiled=True, axis_index_groups=far_groups
        )

    def home_parts(parts):
        own = lax.dynamic_index_in_dim(parts, k, 0, keepdims=False)
        far = lax.dynamic_index_in_dim(parts, 1 - k, 0, keepdims=False)
        return swap(own), swap_far(far)

    def whole_of(home):
        return home[0].astype(F32) + home[1].astype(F32)

    def weight_grad(a, b):
        return with_layout_constraint(tn(a, b).astype(BF16), Layout((0, 1)))

    def slice_at(place):
        number = (place & 1) << top
        place >>= 1
        for bit_number in rest:
            number |= (place & 1) << bit_number
            place >>= 1
        return number | (place << 1)

    order = [slice_at(place) for place in range(seq_size)]
    order_back = [order.index(i) for i in range(seq_size)]

    def arrange(value, order_here):
        return jnp.concatenate(
            [value[..., i * slice_rows : (i + 1) * slice_rows] for i in order_here], -1
        )

    def tie(*values):
        return lax.optimization_barrier(values)

    def after(value, *anchors):
        return tie(value, *anchors)[0]

    def gather_pieces(value):
        pieces = [value]
        for mask in hop_rest + [hop_c]:
            pieces = pieces + [hop(p, mask) for p in pieces]
        return pieces

    def add_low(a, b):
        return (a.astype(F32) + b.astype(F32)).astype(BF16)

    def spread(value, beside=(), later=()):
        half = value.shape[0] // 2
        by_x, by_w = hop(value, hop_x), hop(value, hop_w)
        if beside:
            by_x, by_w, beside = tie(by_x, by_w, beside)
        far = (hop(by_w[:half], hop_x), hop(by_x[half:], hop_w))
        if later:
            far, later = tie(far, later)
        whole = join((value, by_x, by_w) + far)
        return (whole, *beside, *later) if beside or later else whole

    def collect(values, weight, first, count, beside=(), later=()):
        own, to_x, to_w, far_x, far_w = project_out(values, weight, first, count)
        from_x, from_w = hop(far_x, hop_x), hop(far_w, hop_w)
        if beside:
            from_x, from_w, beside = tie(from_x, from_w, beside)
        kinds = [shape_of(*to_x.shape, BF16)] * 2
        to_x, to_w = vmem_call(fold_kernel, kinds, (to_x, to_w, from_x, from_w), "fold")
        got_x, got_w = hop(to_x, hop_x), hop(to_w, hop_w)
        if later:
            got_x, got_w, later = tie(got_x, got_w, later)
        return ((own, got_x, got_w), *beside, *later)

    def lines_of(value):
        return (value,) + tuple(hop(value, m) for m in hop_group[1:])

    def text_sum(value):
        total = value
        half_rows = value.shape[-1] // 2
        for j in (1, 2, 3):
            other = hop(value, hop_group[j])
            if j > 1:
                other = jnp.concatenate((other[..., half_rows:], other[..., :half_rows]), -1)
            total = total + other
        return total

    def all_sum(value, masks):
        for mask in masks:
            value = value.astype(BF16)
            value = value.astype(F32) + hop(value, mask).astype(F32)
        return value

    def by_home(own, other):
        return jnp.where(c == w, own, other)

    piece = tok_rows // 4
    group_rows = 8 * piece
    share_rows = 2 * piece

    def take_share(array):
        parts = array.reshape(micros, 4, piece, width)
        pick = lambda micro: arrange(
            lax.dynamic_index_in_dim(
                lax.dynamic_index_in_dim(parts, micro, 0, keepdims=False), t, 0, keepdims=False
            ),
            order,
        )
        return jnp.concatenate((pick(k), hop(pick(1 - k), hop_k)), 0)

    def give_far(share):
        rows_each = share.shape[0] // 2
        share = arrange(share, order_back)
        own, far = share[:rows_each], hop(share[rows_each:], hop_k)
        return jnp.where(k == 0, jnp.stack((own, far)), jnp.stack((far, own)))

    def give_far_two(one, two):
        one, two = arrange(one, order_back), arrange(two, order_back)
        size, size_two = one.shape[0] // 2, two.shape[0] // 2
        far = hop(jnp.concatenate((one[size:], two[size_two:]), 0), hop_k)
        own = jnp.concatenate((one[:size], two[:size_two]), 0)
        return jnp.where(k == 0, jnp.stack((own, far)), jnp.stack((far, own)))

    def give_across(both):
        return both, hop(both, hop_x)

    def give_back(both, across, position):
        rows_each = both.shape[1]
        pieces = ((0, both), (1, hop(both, hop_c)), (2, across), (3, hop(across, hop_c)))
        out = jnp.zeros((micros, 4, rows_each, width), both.dtype)
        for offset, value in pieces:
            out = lax.dynamic_update_index_in_dim(out, value, position(t ^ offset), 1)
        return out.reshape(micros, 4 * rows_each, width)

    state_in = take_share(inputs)
    meta = jnp.stack((latent_ids, pad_mask, frame_pos, row_pos, col_pos))[None]
    meta = jnp.concatenate((meta, hop(meta, hop_k)), 0)

    def by_own(value, axis):
        value = jnp.where(x == 1, jnp.flip(value, axis), value)
        return jnp.where(c == 1, jnp.flip(value, axis + 1), value)

    ids_share = lax.dynamic_index_in_dim(meta[:, 0], k, 1, keepdims=False)
    ids_share = by_own(ids_share.reshape(2, 2, 2, piece), 1)[:, 0, 0].reshape(-1)[:, None]
    table = modulation + lax.dynamic_index_in_dim(timestep_emb, k, 0, keepdims=False)
    vectors = arrange(
        jnp.concatenate(
            (
                table.reshape(latents * 6, width),
                out_bias.astype(F32),
                cross_norm_gain[None].astype(F32),
                cross_norm_bias[None].astype(F32),
            ),
            0,
        ),
        order,
    )
    (
        share_first,
        share_top,
        share_middle,
        share_last,
        share_result,
        share_back_last,
        share_back_middle,
        share_back_first,
    ) = share_kernels(latents)
    share_low = shape_of(share_rows, width, BF16)
    share_full = shape_of(share_rows, width)
    sums_shape = lambda count: shape_of(count, width)
    (act_share,) = vmem_call(
        share_first, [share_low], (state_in, ids_share, vectors), "share_first"
    )

    pack = lambda a: a.transpose(1, 0, 2).reshape(slice_rows, -1)
    placed_first = place_weight(pack(attn_in))
    act_low = spread(act_share)
    w_first = gather_weight(placed_first)
    grad_top = take_share(after(cotangent, act_low))
    (top_share,) = vmem_call(share_top, [share_low], (grad_top, ids_share, vectors), "share_top")
    second_block = jnp.concatenate((attn_out.T, pack(cross_in[1:])), 1)
    placed_second = place_weight(after(second_block, act_low))
    mid_block = jnp.concatenate((cross_in[0], cross_out.T), 1)
    meta = after(meta, act_low)
    for mask in [hop_w] + hop_rest:
        meta = jnp.concatenate((meta, hop(meta, mask)), 0)
    meta = lax.dynamic_index_in_dim(meta, k, 2, keepdims=False)
    meta = by_own(meta.reshape((2,) * bits + (5, 2, 2, piece)), bits + 1)
    others = list(range(bits - 2))
    meta = meta.transpose([bits, bits + 2] + others + [bits - 2, bits + 1, bits - 1, bits + 3])
    meta = meta.reshape(5, -1)
    ids_all = meta[0]
    key_code = jnp.where(meta[1] == 1, ids_all, -1)
    ids_here = ids_all[:group_rows]
    cosine, signed = rope_tables(*(meta[i, :group_rows] for i in (2, 3, 4)))

    flat = jnp.concatenate((in_bias.reshape(-1), norm_gains.reshape(-1), ffn_bias))
    flat = by_home(flat, hop(flat, hop_c)).astype(F32)
    bias_in = flat[: 6 * columns].reshape(2, 3, columns)
    gains = flat[6 * columns : 10 * columns].reshape(4, columns)
    bias_ffn = flat[10 * columns :]

    half = text_rows // 2
    texts = text_states.reshape(micros, 2, half, width)

    def text_of(micro):
        own = lax.dynamic_index_in_dim(
            lax.dynamic_index_in_dim(texts, micro, 0, keepdims=False), c, 0, keepdims=False
        )
        return arrange(own, order)

    text_here = jnp.concatenate(
        (text_of(k), hop(after(text_of(1 - k), act_low), hop_k)), 0
    )
    number = jnp.arange(4 * half * seq_size // 2, dtype=jnp.int32)
    row, chunk = number % half, number // half
    row_k, row_w, row_rest = chunk & 1, (chunk >> 1) & 1, chunk >> 2
    place = ((row_k ^ k) << top) | ((row_w ^ w) << 1)
    for i, b in enumerate(rest):
        place = place | ((((row_rest >> i) & 1) ^ seq_bit(b)) << b)
    row_c = (row_rest >> len(rest)) ^ c
    text_code = (place * text_rows + row_c * half + row) // TXT

    projected = nn(act_low, w_first) + bias_in[0].reshape(1, -1)
    w_second = gather_weight(after(placed_second, projected))
    w_attn_out, w_text = w_second[:, :columns], w_second[:, columns:]
    placed_mid = place_weight(after(mid_block, projected))
    lines = lines_of(squares(projected, columns, 2))
    query_low, pair, inverse = shape_heads(projected, lines, gains, cosine, signed, width)
    grad_branch_three = spread(after(top_share, pair))
    swapped_up = swap(after(ffn_in, pair))
    text_near = after(text_here, pair)
    text_here = jnp.concatenate((text_near, hop(text_near, hop_w)), 0)
    pairs = gather_pieces(pair)
    pairs, placed_mid, swapped_up, grad_branch_three, text_here = tie(
        pairs, placed_mid, swapped_up, grad_branch_three, text_here
    )
    text_pre = nn(text_here, w_text) + bias_in[1, 1:].reshape(1, -1)
    ckey_pre = text_pre[:, :columns]
    text_squares = text_sum(jnp.sum(ckey_pre * ckey_pre, -1)[None])[0]
    inverse_ck = lax.rsqrt(text_squares / width + EPS)[:, None]
    text_pair = jnp.concatenate(
        (
            (ckey_pre * inverse_ck * gains[3]).astype(BF16),
            text_pre[:, columns:].astype(BF16),
        ),
        1,
    )
    w_mid = gather_weight(placed_mid)
    w_up = gather_far(swapped_up)
    text_pairs = gather_pieces(after(text_pair, pairs))
    attn_full, attn_low, attn_lines = attend(query_low, pairs, ids_here, key_code, True)
    (parts,) = collect(attn_low, w_second, 0, columns)
    swapped_down = swap(after(ffn_out.T, parts))
    state_one, branch_one, cross_share = vmem_call(
        share_middle,
        [share_full, share_full, share_low],
        (*parts, state_in, ids_share, vectors),
        "share_middle",
    )

    cross_act, text_pairs, swapped_down = spread(cross_share, (text_pairs,), (swapped_down,))
    w_down = gather_far(swapped_down)
    cquery_pre = nn(cross_act, w_mid[:, :columns]) + bias_in[1, 0]
    cross_lines_here = lines_of(squares(cquery_pre, columns, 1))
    cquery_low, inverse_cq = shape_cross(cquery_pre, cross_lines_here, gains, width)
    cross_full, cross_low, total_lines = attend(
        cquery_low, text_pairs, ids_here, text_code, False
    )
    (parts,) = collect(cross_low, w_mid, columns, columns)
    state_two, ffn_share = vmem_call(
        share_last,
        [share_full, share_low],
        (*parts, state_one, ids_share, vectors),
        "share_last",
    )

    ffn_act = spread(ffn_share)
    hidden_pre = nn(ffn_act, w_up) + bias_ffn
    hidden_low = jax.nn.gelu(hidden_pre, approximate=True).astype(BF16)

    gelu_pull = jax.vjp(lambda h: jax.nn.gelu(h, approximate=True), hidden_pre)[1]
    grad_hidden = gelu_pull(nn(grad_branch_three, w_down))[0].astype(BF16)
    part_down = weight_grad(grad_branch_three, hidden_low)
    part_up = weight_grad(ffn_act, grad_hidden)
    half_up = scatter_weight(part_up)
    parts, part_down, part_up = collect(
        grad_hidden, w_up, 0, hidden, (part_down,), (part_up,)
    )
    grad_two, gb2_share, sums_two = vmem_call(
        share_back_last,
        [share_full, share_low, sums_shape(2 * latents + 2)],
        (*parts, state_two, grad_top, top_share, ids_share, vectors),
        "share_back_last",
    )

    half_down = scatter_far(after(part_down, gb2_share))
    grad_branch_two = spread(gb2_share)
    out_parts, = collect(after(hidden_low, gb2_share), w_down, 0, hidden)
    out_share, sums_three = vmem_call(
        share_result,
        [share_low, sums_shape(latents)],
        (*out_parts, state_two, grad_top, ids_share, vectors),
        "share_result",
    )
    grad_cross = nn(grad_branch_two, w_mid[:, columns:]).astype(BF16)
    hidden_half = hidden // 2
    grad_cquery, text_near, text_far = attend_back(
        cquery_low,
        grad_cross,
        cross_full,
        total_lines,
        text_pairs,
        ids_here,
        text_code,
        False,
    )
    back_lines = lines_of(cross_lines(grad_cquery, cquery_pre, gains))
    text_far = hop(text_far, hop_c)
    back_lines, text_far = tie(back_lines, text_far)
    gcq_low, sums_cq = back_cross(
        grad_cquery, cquery_pre, inverse_cq, back_lines, gains, width
    )
    gpair = add_low(text_near, text_far)
    for mask in hop_rest[::-1]:
        rows_left = gpair.shape[0] // 2
        gpair = add_low(gpair[:rows_left], hop(gpair[rows_left:], mask))
    parts, gpair, out_share = collect(gcq_low, w_mid, 0, columns, (gpair,), (out_share,))
    grad_one, gb1_share, sums_one = vmem_call(
        share_back_middle,
        [share_full, share_low, sums_shape(latents + 3)],
        (*parts, state_one, grad_two, branch_one, ids_share, vectors),
        "share_back_middle",
    )

    gckey = gpair[:, :columns].astype(F32)
    sums_ck = text_sum(jnp.sum(gains[3] * gckey * ckey_pre, -1)[None])[0]
    out_both = give_far(out_share)
    grad_branch_one, sums_ck, out_both = spread(gb1_share, (sums_ck,), (out_both,))
    home_up = home_parts(after(half_up, out_both))
    out_both, out_across = give_across(out_both)
    gck_low = rms_pull(ckey_pre, inverse_ck, gains[3], gckey, sums_ck[:, None], width)
    gtext = jnp.concatenate((gck_low, gpair[:, columns:]), 1)
    text_part = nt(gtext, w_text).astype(BF16)
    text_back = hop(text_part[2 * half :], hop_w)

    grad_attn = nn(grad_branch_one, w_attn_out).astype(BF16)
    part_mid = jnp.concatenate(
        (
            weight_grad(text_here, gtext),
            weight_grad(grad_branch_one, attn_low),
            weight_grad(cross_act, gcq_low),
            weight_grad(grad_branch_two, cross_low),
        ),
        1,
    )
    half_mid = scatter_weight(part_mid)
    grad_attn, text_back, out_across = tie(grad_attn, text_back, out_across)
    grad_query, near, far = attend_back(
        query_low, grad_attn, attn_full, attn_lines, pairs, ids_here, key_code, True
    )
    far = hop(far, hop_c)
    kv_back = add_low(near, far)
    for mask in hop_rest[::-1]:
        rows_left = kv_back.shape[0] // 2
        kv_back = add_low(kv_back[:rows_left], hop(kv_back[rows_left:], mask))
    kv_back, home_up = tie(kv_back, home_up)
    gquery, gkey, head_lines = turn_back(
        grad_query, kv_back, projected, gains, cosine, signed
    )
    head_lines = lines_of(head_lines)
    text_sub = half // 2
    text_part = text_part[: 2 * half].astype(F32) + text_back.astype(F32)
    text_part = text_part.reshape(2, 2, text_sub, width)
    text_share = lax.dynamic_index_in_dim(text_part, x, 1, keepdims=False)
    text_given = lax.dynamic_index_in_dim(text_part, 1 - x, 1, keepdims=False)
    text_got = hop(text_given.astype(BF16), hop_x)
    block_out = give_back(out_both, out_across, lambda place_here: place_here)
    head_lines, text_got, block_out = tie(head_lines, text_got, block_out)
    text_share = (text_share + text_got.astype(F32)).astype(BF16)
    grad_proj, sums_heads = back_heads(
        gquery, gkey, projected, inverse, kv_back, head_lines, gains, width
    )
    part_attn = weight_grad(act_low, grad_proj)
    part_whole = part_attn
    part_attn = part_attn.reshape((2,) * (bits - 1) + (2, slice_rows, 3 * columns))
    steps = [(0, hop_c, c)] + [
        (1 + i, tensor_size << b, seq_bit(b)) for i, b in enumerate(rest[::-1])
    ]
    given = hop(lax.dynamic_index_in_dim(part_attn, 1 - c, 0, keepdims=True), hop_c)
    part_attn = add_low(lax.dynamic_index_in_dim(part_attn, c, 0, keepdims=True), given)
    part_near = part_attn
    for axis, mask, mine in steps[1:]:
        kept = lax.dynamic_index_in_dim(part_attn, mine, axis, keepdims=True)
        given = lax.dynamic_index_in_dim(part_attn, 1 - mine, axis, keepdims=True)
        part_attn = add_low(kept, hop(given, mask))
    part_attn = part_attn.reshape(2, slice_rows, 3 * columns)
    parts, part_near, part_attn = collect(
        after(grad_proj, part_whole), w_first, 0, 3 * columns, (part_near,), (part_attn,)
    )
    home_down = swap(after(half_down, parts))
    grad_share, sums_zero = vmem_call(
        share_back_first,
        [share_low, sums_shape(2 * latents)],
        (*parts, state_in, grad_one, ids_share, vectors),
        "share_back_first",
    )
    rows_sum = lambda a: jnp.sum(a.astype(F32), 0)
    extra = -hidden % columns
    column_sums = jnp.concatenate(
        (
            sums_heads[0].reshape(3, columns),
            sums_cq[:1],
            rows_sum(gtext).reshape(2, columns),
            sums_heads[1, : 2 * columns].reshape(2, columns),
            sums_cq[1:2],
            rows_sum(gckey * ckey_pre * inverse_ck)[None],
            jnp.pad(rows_sum(grad_hidden), (0, extra)).reshape(-1, columns),
        ),
        0,
    )
    count = latents
    feature_sums = jnp.concatenate(
        (
            sums_zero,
            sums_one[:count],
            sums_two[: 2 * count],
            sums_three,
            sums_one[count : count + 1],
            sums_two[2 * count :],
            sums_one[count + 1 :],
        ),
        0,
    )
    marks = column_sums.shape[0]
    lanes = width // columns
    column_sums = jnp.pad(column_sums, ((0, -marks % lanes), (0, 0))).reshape(-1, width)
    features = feature_sums.shape[0]
    near_sums = jnp.concatenate((feature_sums, column_sums), 0).astype(BF16)
    far_sums = hop(near_sums, hop_k)
    text_share = text_share.reshape(2 * text_sub, width)
    both = give_far_two(grad_share, text_share)
    home_attn = home_parts(after(part_attn, both, far_sums))
    home_mid = home_parts(after(half_mid, both, far_sums))
    across = hop(both, hop_x)
    returned = ((0, both), (1, hop(both, hop_c)), (2, across), (3, hop(across, hop_c)))

    def put_back(first, rows_each, position):
        out = jnp.zeros((micros, 4, rows_each, width), BF16)
        for offset, value in returned:
            out = lax.dynamic_update_index_in_dim(
                out, value[:, first : first + rows_each], position(t ^ offset), 1
            )
        return out.reshape(micros, 4 * rows_each, width).astype(F32)

    grad_inputs = put_back(0, piece, lambda place_here: place_here)
    grad_text = put_back(
        piece, text_sub, lambda place_here: ((place_here & 1) << 1) | (place_here >> 1)
    )
    grad_attn_in = whole_of(home_attn)
    grad_mid = whole_of(home_mid)
    grad_up = whole_of(home_up)
    grad_down = home_down.astype(F32)

    column_sums = near_sums[features:].astype(F32) + far_sums[features:].astype(F32)
    sums = jnp.concatenate(
        (near_sums[:features].astype(F32), far_sums[:features].astype(F32), column_sums), 0
    )
    sums = all_sum(sums, [hop_c])
    feature_sums = all_sum(sums[: 2 * features], [hop_x, hop_w])
    sums = all_sum(jnp.concatenate((feature_sums, sums[2 * features :]), 0), hop_rest)
    sums = sums.astype(BF16)
    column_sums = sums[2 * features :]
    column_sums = by_home(column_sums, hop(column_sums, hop_w)).astype(F32)
    column_sums = column_sums.reshape(-1, columns)[:marks]
    grad_in_bias = column_sums[:6].reshape(2, 3, columns)
    grad_gains = column_sums[6:10]
    grad_ffn_bias = column_sums[10:].reshape(-1)[:hidden]

    near_features = arrange(sums[:features], order_back).astype(F32)
    far_features = arrange(sums[features : 2 * features], order_back).astype(F32)
    both_sums = near_features + far_features
    count = 6 * latents
    near_temb = near_features[:count].reshape(6, latents, width).transpose(1, 0, 2)
    far_temb = far_features[:count].reshape(6, latents, width).transpose(1, 0, 2)
    grad_temb = jnp.where(
        k == 0, jnp.stack((near_temb, far_temb)), jnp.stack((far_temb, near_temb))
    )
    grad_mod = jnp.sum(grad_temb, (0, 1))

    unpack = lambda a: a.reshape(slice_rows, -1, columns).transpose(1, 0, 2)
    part = lambda i: grad_mid[:, i * columns : (i + 1) * columns]
    return (
        block_out,
        grad_inputs,
        grad_text,
        grad_temb,
        grad_mod,
        unpack(grad_attn_in),
        grad_in_bias,
        grad_gains,
        part(2).T,
        jnp.stack((part(3), part(0), part(1))),
        part(4).T,
        both_sums[count + 3],
        both_sums[count + 4],
        grad_up,
        grad_ffn_bias,
        grad_down.T,
        both_sums[count : count + 3],
    )


def solution(mesh):
    placed = (
        P(None, "seq", None),
        P(None, "seq", None),
        P(),
        P(),
        P(None, "seq", "tensor"),
        P(None, None, "tensor"),
        P(None, "tensor"),
        P("tensor", "seq"),
        P(None, "seq", "tensor"),
        P("tensor", "seq"),
        P(),
        P(),
        P("seq", "tensor"),
        P("tensor"),
        P("tensor", "seq"),
        P(),
        P(None, "seq"),
        P(None, "seq"),
        P(None, "seq"),
        P(None, "seq"),
        P(None, "seq"),
        P(None, "seq", None),
    )
    return jax.shard_map(
        shards,
        mesh=mesh,
        in_specs=placed,
        out_specs=(
            P(None, "seq", None),
            P(None, "seq", None),
            P(None, "seq", None),
            P(),
            P(),
            P(None, "seq", "tensor"),
            P(None, None, "tensor"),
            P(None, "tensor"),
            P("tensor", "seq"),
            P(None, "seq", "tensor"),
            P("tensor", "seq"),
            P(),
            P(),
            P("seq", "tensor"),
            P("tensor"),
            P("tensor", "seq"),
            P(),
        ),
        check_vma=False,
    )
```
